768 devices in a mesh: scene: 96 (over z, x, core), seq: 8 (over y).
Axes of the slice: x: 4, y: 8, z: 12, core: 2. Of those that a mesh axis runs over, the one named last changes fastest.
Arguments:
- qkv: bfloat16 [3, 98304, 1280], P(None, ('scene', 'seq')), may hold values from -6.5 to 6.5
- view_counts: int32 [96], P('scene'), may hold values from 1 to 2, as said below
- out_weight: bfloat16 [1280, 1280], replicated, may hold values from -0.15625 to 0.15625
- out_cotangent: bfloat16 [98304, 1280], P(('scene', 'seq')), may hold values from -6 to 6
Outputs:
- d_qkv: bfloat16 [3, 98304, 1280], P(None, ('scene', 'seq'))
- weight_grad: float32 [1280, 1280], P('seq')
The draws below stay inside these ranges and needn't reach their ends.
Inputs may be any that keep to these rules, and one draw needn't show every extreme that they name: `view_counts`: some scene has 2 views and some 1.
All inputs are finite; a program needn't handle non-finite values.
Results may differ from the reference program's by a relative error of at most 0.0065.
Values may be sent and summed in bfloat16 or wider, within the bound.
A program may use at most 64 MiB of HBM per device.

```python
import math
import jax
import jax.numpy as jnp
from jax import lax

D = 1280
HD = 64
HV = 12
TV = 512
VMAX = 2
VMIN = 1
SCENES = 96
TOKENS = 98304


def draw_qkv(key, part):
    total = SCENES * VMAX * TV
    base_key = jax.random.fold_in(jax.random.fold_in(key, 11), 0)
    base = jax.random.truncated_normal(base_key, -6.0, 6.0, (3, total, D), jnp.float32)
    return base.astype(jnp.bfloat16)


def draw_view_counts(key, part):
    first, second, third = jax.random.split(jax.random.fold_in(key, 13), 3)
    counts = jax.random.randint(first, (SCENES,), VMIN, VMAX + 1)
    top_at = jax.random.randint(second, (), 0, SCENES)
    low_at = (top_at + 1 + jax.random.randint(third, (), 0, SCENES - 1)) % SCENES
    counts = counts.at[top_at].set(VMAX).at[low_at].set(VMIN)
    return counts.astype(jnp.int32)


def block_scale(rng, extent, shards, low, top_value):
    gain, own = 1.0, jax.random.fold_in(rng, 6)
    for position, parts in shards:
        heights = jnp.exp(jax.random.uniform(jax.random.fold_in(own, position), (parts,), jnp.float32, low / len(shards), top_value / len(shards)))
        gain = gain * jnp.repeat(heights, extent[position] // parts).reshape([-1 if axis == position else 1 for axis in range(len(extent))])
    return gain


def gaussian(own_key, shape, scale, bound, cuts=(), held_as=jnp.bfloat16):
    loudness = block_scale(own_key, shape, cuts, -0.22, 0.18) if cuts else 1.0
    array = jax.random.normal(own_key, shape, jnp.float32) * scale * loudness
    return jnp.minimum(jnp.maximum(array, -bound), bound).astype(held_as)


def setup_inputs(seed: int = 0) -> dict:
    seeds = jax.random.split(jax.random.key(seed), 5)
    return {
        "qkv": draw_qkv(jax.random.fold_in(seeds[4], 71), 0),
        "view_counts": draw_view_counts(jax.random.fold_in(seeds[4], 71), 0),
        "out_weight": gaussian(seeds[2], (D, D), D ** -0.5, 0.15625),
        "out_cotangent": gaussian(seeds[3], (TOKENS, D), 1.0, 6.0, ((0, 768),)),
    }


def attend(queries, keys, values, key_live, query_live):
    scale = 1.0 / math.sqrt(queries.shape[-1])
    scores = jnp.einsum('blhd,bmhd->bhlm', queries.astype(jnp.float32), keys.astype(jnp.float32)) * scale
    scores = jnp.where(key_live[:, None, None, :] > 0.5, scores, -1e+30)
    probs = jax.nn.softmax(scores, axis=-1)
    rounded = lax.optimization_barrier(probs.astype(jnp.bfloat16))
    outputs = jnp.einsum('bhlm,bmhd->blhd', rounded.astype(jnp.float32), values.astype(jnp.float32))
    return (outputs * query_live[:, :, None, None], probs, rounded)

def attend_back(queries, keys, values, probs, rounded, query_live, grad_out):
    scale = 1.0 / math.sqrt(queries.shape[-1])
    grad_in = grad_out.astype(jnp.float32) * query_live[:, :, None, None]
    grad_values = jnp.einsum('bhlm,blhd->bmhd', rounded.astype(jnp.float32), grad_in)
    grad_probs = jnp.einsum('blhd,bmhd->bhlm', grad_in, values.astype(jnp.float32))
    grad_scores = probs * (grad_probs - lax.optimization_barrier(jnp.sum(probs * grad_probs, axis=-1, keepdims=True))) * scale
    grad_queries = jnp.einsum('bhlm,bmhd->blhd', grad_scores, keys.astype(jnp.float32))
    grad_keys = jnp.einsum('bhlm,blhd->bmhd', grad_scores, queries.astype(jnp.float32))
    return jnp.stack([grad_queries, grad_keys, grad_values]).astype(jnp.bfloat16)

def reference(qkv, view_counts, out_weight, out_cotangent):
    width = qkv.shape[2]
    view_width = HV * HD
    cross_width = width - view_width
    cross_heads = cross_width // HD
    group = VMAX * TV
    all_qkv = qkv.reshape(3, SCENES, TV, VMAX, width).transpose(1, 0, 2, 3, 4)
    cot_all = out_cotangent.reshape(SCENES, group, width)

    def one_scene(grad_sum, scene):
        part, view_count, cotangent = scene
        live = (jnp.arange(VMAX) < view_count).astype(jnp.float32)
        grad_out = lax.dot_general(cotangent, out_weight, (((1,), (1,)), ((), ())), preferred_element_type=jnp.float32).astype(jnp.bfloat16)
        grad_out = grad_out.reshape(TV, VMAX, width)
        per = part[..., :view_width].reshape(3, TV, VMAX, HV, HD).transpose(0, 2, 1, 3, 4)
        view_keep = jnp.broadcast_to(live[:, None], (VMAX, TV))
        all_keys = jnp.ones((VMAX, TV), jnp.float32)
        view_out, view_probs, view_rounded = attend(per[0], per[1], per[2], all_keys, view_keep)
        view_grad_in = grad_out[..., :view_width].reshape(TV, VMAX, HV, HD).transpose(1, 0, 2, 3)
        view_grads = attend_back(per[0], per[1], per[2], view_probs, view_rounded, view_keep, view_grad_in)
        view_grads = view_grads.transpose(0, 2, 1, 3, 4).reshape(3, TV, VMAX, view_width)
        view_flat = view_out.astype(jnp.bfloat16).transpose(1, 0, 2, 3).reshape(TV, VMAX, view_width)
        cross = part[..., view_width:].reshape(3, TV, VMAX, cross_heads, HD)
        cross_keep = jnp.broadcast_to(live[None, :], (TV, VMAX))
        cross_out, cross_probs, cross_rounded = attend(cross[0], cross[1], cross[2], cross_keep, cross_keep)
        cross_grad_in = grad_out[..., view_width:].reshape(TV, VMAX, cross_heads, HD)
        cross_grads = attend_back(cross[0], cross[1], cross[2], cross_probs, cross_rounded, cross_keep, cross_grad_in).reshape(3, TV, VMAX, cross_width)
        cross_flat = cross_out.astype(jnp.bfloat16).reshape(TV, VMAX, cross_width)
        attn_flat = jnp.concatenate([view_flat, cross_flat], axis=-1).reshape(group, width)
        step_grad = jnp.dot(attn_flat.T, cotangent, preferred_element_type=jnp.float32)
        grads = jnp.concatenate([view_grads, cross_grads], axis=-1).reshape(3, group, width)
        return (grad_sum + step_grad, grads)
    grad_sum, stacked = lax.scan(one_scene, jnp.zeros((width, width), jnp.float32), (all_qkv, view_counts, cot_all))
    weight_grad = grad_sum * (1.0 / math.sqrt(TOKENS))
    d_qkv = stacked.transpose(1, 0, 2, 3).reshape(3, TOKENS, width)
    return (d_qkv, weight_grad)
```

```python
import math

import jax
import jax.numpy as jnp
from jax import lax
from jax.sharding import PartitionSpec as P

HD = 64
HV = 12
TV = 512
VMAX = 2


def attend(queries, keys, values, key_live, query_live):
    scale = 1.0 / math.sqrt(queries.shape[-1])
    scores = (
        jnp.einsum("blhd,bmhd->bhlm", queries, keys, preferred_element_type=jnp.float32) * scale
    )
    scores = jnp.where(key_live[:, None, None, :] > 0.5, scores, -1e30)
    probs = jax.nn.softmax(scores, axis=-1)
    rounded = probs.astype(jnp.bfloat16)
    outputs = jnp.einsum("bhlm,bmhd->blhd", rounded, values, preferred_element_type=jnp.float32)
    return (outputs * query_live[:, :, None, None], probs, rounded)


def attend_back(queries, keys, values, probs, rounded, query_live, grad_out):
    scale = 1.0 / math.sqrt(queries.shape[-1])
    grad_in = grad_out * query_live[:, :, None, None].astype(jnp.bfloat16)
    grad_values = jnp.einsum(
        "bhlm,blhd->bmhd", rounded, grad_in, preferred_element_type=jnp.float32
    )
    grad_probs = jnp.einsum("blhd,bmhd->bhlm", grad_in, values, preferred_element_type=jnp.float32)
    grad_scores = probs * (grad_probs - jnp.sum(probs * grad_probs, axis=-1, keepdims=True)) * scale
    grad_queries = jnp.einsum("bhlm,bmhd->blhd", grad_scores, keys.astype(jnp.float32))
    grad_keys = jnp.einsum("bhlm,blhd->bmhd", grad_scores, queries.astype(jnp.float32))
    return jnp.stack([grad_queries, grad_keys, grad_values]).astype(jnp.bfloat16)


def on_device(qkv, view_counts, out_weight, out_cotangent):
    width = qkv.shape[2]
    tok_rows = qkv.shape[1]
    seq_parts = lax.axis_size("seq")
    seq_index = lax.axis_index("seq")
    places = tok_rows // VMAX
    groups = seq_parts // VMAX
    view_width = HV * HD
    group_width = view_width // groups
    group_heads = HV // groups
    cross_width = width - view_width
    cross_heads = cross_width // HD
    view_count = view_counts[0]
    live_all = (jnp.arange(VMAX) < view_count).astype(jnp.float32)
    local = qkv.reshape(3, places, VMAX, width)
    view_part = local[..., :view_width].reshape(3, places, VMAX * groups, group_width)
    contract_last = (((1,), (1,)), ((), ()))
    grad_all = lax.dot_general(
        out_cotangent, out_weight, contract_last, preferred_element_type=jnp.float32
    ).astype(jnp.bfloat16)
    grad_view = grad_all[:, :view_width].reshape(1, places, VMAX * groups, group_width)
    arrived, grad_arrived = (
        lax.all_to_all(view_part, "seq", split_axis=2, concat_axis=1, tiled=True),
        lax.all_to_all(grad_view, "seq", split_axis=2, concat_axis=1, tiled=True),
    )
    my_view = seq_index // groups
    view_live = (my_view < view_count).astype(jnp.float32)
    query_live = jnp.broadcast_to(view_live, (1, TV))
    all_keys = jnp.ones((1, TV), jnp.float32)
    heads_in = arrived.reshape(3, TV, group_heads, HD).transpose(2, 0, 1, 3)
    grad_heads = grad_arrived.reshape(TV, group_heads, HD).transpose(1, 0, 2)

    def one_head(item):
        stacked, grad_one = item
        queries = stacked[0][None, :, None, :]
        keys = stacked[1][None, :, None, :]
        values = stacked[2][None, :, None, :]
        out_one, probs, rounded = attend(queries, keys, values, all_keys, query_live)
        grads = attend_back(
            queries, keys, values, probs, rounded, query_live, grad_one[None, :, None, :]
        )
        return (out_one.astype(jnp.bfloat16)[0, :, 0, :], grads[:, 0, :, 0, :])

    head_outs, head_grads = lax.map(one_head, (heads_in, grad_heads))
    view_out = head_outs.transpose(1, 0, 2).reshape(1, TV, 1, group_width)
    view_grads = head_grads.transpose(1, 2, 0, 3).reshape(3, TV, 1, group_width)
    grads_home, out_home = (
        lax.all_to_all(view_grads, "seq", split_axis=1, concat_axis=2, tiled=True),
        lax.all_to_all(view_out, "seq", split_axis=1, concat_axis=2, tiled=True),
    )
    grads_home = grads_home.reshape(3, places, VMAX, view_width)
    out_home = out_home.reshape(places, VMAX, view_width)
    cross = local[..., view_width:].reshape(3, places, VMAX, cross_heads, HD)
    cross_keep = jnp.broadcast_to(live_all[None, :], (places, VMAX))
    cross_out, cross_probs, cross_rounded = attend(
        cross[0], cross[1], cross[2], cross_keep, cross_keep
    )
    cross_grad_in = grad_all[:, view_width:].reshape(places, VMAX, cross_heads, HD)
    cross_grads = attend_back(
        cross[0], cross[1], cross[2], cross_probs, cross_rounded, cross_keep, cross_grad_in
    ).reshape(3, places, VMAX, cross_width)
    cross_flat = cross_out.astype(jnp.bfloat16).reshape(places, VMAX, cross_width)
    attn_flat = jnp.concatenate([out_home, cross_flat], axis=-1).reshape(tok_rows, width)
    d_qkv = jnp.concatenate([grads_home, cross_grads], axis=-1).reshape(3, tok_rows, width)
    feature_cols = lax.all_to_all(attn_flat, "seq", split_axis=1, concat_axis=0, tiled=True)
    contract_first = (((0,), (0,)), ((), ()))
    grad_rows = lax.dot_general(
        feature_cols,
        lax.all_gather(out_cotangent, "seq", axis=0, tiled=True),
        contract_first,
        preferred_element_type=jnp.float32,
    )
    scenes = lax.axis_size("scene")
    scale = 1.0 / math.sqrt(scenes * seq_parts * tok_rows)
    rows = grad_rows.shape[0]
    per = -(-rows // scenes)
    padded = jnp.pad(grad_rows, ((0, per * scenes - rows), (0, 0))).astype(jnp.bfloat16)
    pieces = lax.all_to_all(
        padded.reshape(scenes, per, width), "scene", split_axis=0, concat_axis=0, tiled=True
    )
    part = (jnp.sum(pieces.astype(jnp.float32), axis=0) * scale).astype(jnp.bfloat16)
    weight_grad = lax.all_gather(part, "scene", axis=0, tiled=True)[:rows].astype(jnp.float32)
    return (d_qkv, weight_grad)


def solution(mesh):
    in_specs = (P(None, ("scene", "seq"), None), P("scene"), P(), P(("scene", "seq"), None))
    out_specs = (P(None, ("scene", "seq"), None), P("seq", None))
    return jax.shard_map(
        on_device, mesh=mesh, in_specs=in_specs, out_specs=out_specs, check_vma=False
    )
```

```python
import functools
import math

import jax
import jax.numpy as jnp
from jax import lax
from jax.experimental import pallas as pl
from jax.experimental.pallas import tpu as pltpu
from jax.sharding import PartitionSpec as P

MESH = pl.DeviceIdType.MESH
F32 = jnp.float32
BF16 = jnp.bfloat16
NT = (((1,), (1,)), ((), ()))
TN = (((0,), (0,)), ((), ()))
NN = (((1,), (0,)), ((), ()))

HD = 64
NY, NX, NZ = 8, 4, 12
GROUPS = 4
HEADS = 3
POS = 64
TV = POS * NY
VIEW_W = 768
CROSS_W = 512
WIDTH = 1280
GW = HEADS * HD
PACK = 640
HALF = WIDTH // 2
BLOCKS = 10
OWNED = 5


def dot(a, b, dims=NN):
    return lax.dot_general(a, b, dims, preferred_element_type=F32)


def kernel(
    vc_ref, qkv_ref, cot_ref, w_ref, d_ref, wg_ref,
    wv, wc, qs, qr, cs, cr, cx, xs, xr, cg, hq, hk, hv, hg, pt, dt, dh, ds, dr, ot,
    ws, wr, wown, x_s, x_r, zown, zs, zr, yb, yr, fc,
    wsem, q_ss, q_rs, c_ss, c_rs, x_ss, x_rs, d_ss, d_rs, own_s, k_ss, k_rs, xx_ss, xx_rs,
    z_ss, z_rs, y_ss, y_rs, za_ss, za_rs, xa_ss, xa_rs, ka_ss, ka_rs,
):
    scene = lax.axis_index("scene")
    y = lax.axis_index("seq")
    c = lax.rem(scene, 2)
    x = lax.rem(lax.div(scene, 2), NX)
    z = lax.div(scene, 2 * NX)
    view = lax.div(y, GROUPS)
    group = lax.rem(y, GROUPS)

    def y_at(d):
        return lax.rem(y + d, NY)

    def z_at(d):
        return lax.rem(z + d, NZ)

    def x_at(d):
        return lax.rem(x + d, NX)

    def to_y(p):
        return {"seq": p}

    def to_scene(zz, xx, cc):
        return {"scene": (zz * NX + xx) * 2 + cc}

    core_peer = to_scene(z, x, 1 - c)

    def remote(src, dst, ssem, rsem, dev):
        return pltpu.make_async_remote_copy(
            src_ref=src, dst_ref=dst, send_sem=ssem, recv_sem=rsem, device_id=dev,
            device_id_type=MESH,
        )

    barrier = pltpu.get_barrier_semaphore()
    peers = [to_y(y_at(d)) for d in range(1, NY)]
    peers += [core_peer]
    peers += [to_scene(z, x_at(d), c) for d in range(1, NX)]
    peers += [to_scene(z_at(d), x, c) for d in range(1, NZ)]
    for peer in peers:
        pl.semaphore_signal(barrier, inc=1, device_id=peer, device_id_type=MESH)
    w_view = pltpu.make_async_copy(
        w_ref.at[pl.ds(pl.multiple_of(group * GW, GW), GW)], wv, wsem.at[0]
    )
    w_cross = pltpu.make_async_copy(w_ref.at[pl.ds(VIEW_W, CROSS_W)], wc, wsem.at[1])
    w_cross.start()
    w_view.start()

    vc = vc_ref[0]
    live = [jnp.where(vc > v, 1.0, 0.0).astype(F32) for v in range(2)]
    my_live = jnp.where(vc > view, 1.0, 0.0).astype(F32)

    row = lax.broadcasted_iota(jnp.int32, (POS, 2 * POS), 0)
    col = lax.broadcasted_iota(jnp.int32, (POS, 2 * POS), 1)
    for v in range(2):
        pick = jnp.where(col == 2 * row + v, 1.0, 0.0).astype(BF16)
        parts = []
        for k in range(3):
            r = dot(pick, qkv_ref[k])
            cx[k, v] = r[:, VIEW_W:]
            parts.append(r[:, :VIEW_W])
        for g in range(GROUPS):
            cols = slice(g * GW, (g + 1) * GW)
            packed = jnp.concatenate(
                [p[:, cols] for p in parts] + [jnp.zeros((POS, PACK - 3 * GW), F32)], axis=1
            )
            qs[v * GROUPS + g] = packed.astype(BF16)
        cs[v] = dot(pick, cot_ref[...]).astype(BF16)

    pl.semaphore_wait(barrier, len(peers))

    def rows_of(ref, p):
        return ref.at[pl.ds(pl.multiple_of(p * POS, POS), POS)]

    def q_copy(d, mine):
        p = y_at(d)
        at = y if mine else p
        return remote(qs.at[p], rows_of(qr, at), q_ss.at[d], q_rs.at[at], to_y(p))

    def c_copy(d, mine):
        p = y_at(d)
        at = y if mine else p
        return remote(
            cs.at[lax.div(p, GROUPS)], rows_of(cr, at), c_ss.at[d], c_rs.at[at], to_y(p)
        )

    def x_copy(d, mine):
        p = y_at(d)
        at = y if mine else p
        return remote(xs.at[p], rows_of(xr, at), x_ss.at[d], x_rs.at[at], to_y(p))

    def d_copy(d, mine):
        p = y_at(d)
        at = y if mine else p
        return remote(rows_of(ds, p), dr.at[at], d_ss.at[d], d_rs.at[at], to_y(p))

    q_own = pltpu.make_async_copy(qs.at[y], rows_of(qr, y), own_s.at[0])
    c_own = pltpu.make_async_copy(cs.at[view], rows_of(cr, y), own_s.at[1])
    x_own = pltpu.make_async_copy(xs.at[y], rows_of(xr, y), own_s.at[2])
    d_own = pltpu.make_async_copy(rows_of(ds, y), dr.at[y], own_s.at[3])

    for d in range(1, NY):
        q_copy(d, True).start()
    q_own.start()
    for d in range(1, NY):
        c_copy(d, True).start()
    c_own.start()

    w_cross.wait()
    same = jnp.where(
        lax.broadcasted_iota(jnp.int32, (CROSS_W, CROSS_W), 0) // HD
        == lax.broadcasted_iota(jnp.int32, (CROSS_W, CROSS_W), 1) // HD,
        1.0,
        0.0,
    ).astype(BF16)

    def head_sum(t):
        hi = t.astype(BF16)
        lo = (t - hi.astype(F32)).astype(BF16)
        return dot(hi, same) + dot(lo, same)

    scale = 1.0 / math.sqrt(HD)
    gs = []
    for v in range(2):
        g = dot(cs[v], wc[...], NT).astype(BF16).astype(F32)
        gs.append(g * live[v])
    dq = []
    dk = [None, None]
    dv = [None, None]
    for a in range(2):
        q = cx[0, a]
        s0 = head_sum(q * cx[1, 0]) * scale
        s1 = head_sum(q * cx[1, 1]) * scale
        s1 = jnp.where(live[1] > 0.5, s1, -1e30)
        m = jnp.maximum(s0, s1)
        e0 = jnp.exp(s0 - m)
        e1 = jnp.exp(s1 - m)
        inv = 1.0 / (e0 + e1)
        p = [e0 * inv, e1 * inv]
        pb = [t.astype(BF16).astype(F32) for t in p]
        out = ((pb[0] * cx[2, 0] + pb[1] * cx[2, 1]) * live[a]).astype(BF16)
        for g in range(GROUPS):
            xs[a * GROUPS + g] = out[:, g * 128 : (g + 1) * 128]
        dp = [head_sum(gs[a] * cx[2, b]) for b in range(2)]
        mean = p[0] * dp[0] + p[1] * dp[1]
        grad = [p[b] * (dp[b] - mean) * scale for b in range(2)]
        dq.append(grad[0] * cx[1, 0] + grad[1] * cx[1, 1])
        for b in range(2):
            tk = grad[b] * q
            tv = pb[b] * gs[a]
            dk[b] = tk if dk[b] is None else dk[b] + tk
            dv[b] = tv if dv[b] is None else dv[b] + tv
    for d in range(1, NY):
        x_copy(d, True).start()
    x_own.start()
    for v in range(2):
        cg[0, v] = dq[v].astype(BF16)
        cg[1, v] = dk[v].astype(BF16)
        cg[2, v] = dv[v].astype(BF16)

    for d in range(1, NY):
        q_copy(d, False).wait_recv()
    q_own.wait()
    packed = qr[...]
    for h in range(HEADS):
        hq[h] = packed[:, h * HD : (h + 1) * HD]
        hk[h] = packed[:, GW + h * HD : GW + (h + 1) * HD]
        hv[h] = packed[:, 2 * GW + h * HD : 2 * GW + (h + 1) * HD]
    w_view.wait()
    for d in range(1, NY):
        c_copy(d, False).wait_recv()
    c_own.wait()
    g_all = (dot(cr[...], wv[...], NT).astype(BF16).astype(F32) * my_live).astype(BF16)
    for h in range(HEADS):
        hg[h] = g_all[:, h * HD : (h + 1) * HD]

    chunk = 128

    def one_head(h, carry):
        k = hk[h]
        v = hv[h]
        for i in range(TV // chunk):
            at = slice(i * chunk, (i + 1) * chunk)
            s = dot(k, hq[h, at, :], NT) * scale
            e = jnp.exp(s - jnp.max(s, axis=0, keepdims=True))
            p = e * (1.0 / jnp.sum(e, axis=0, keepdims=True))
            dp = dot(v, hg[h, at, :], NT)
            mean = jnp.sum(p * dp, axis=0, keepdims=True)
            pt[:, at] = p.astype(BF16)
            dt[:, at] = (p * (dp - mean) * scale).astype(BF16)
        probs = pt[...]
        grads = dt[...]
        ot[pl.ds(pl.multiple_of(h * HD, HD), HD), :] = (dot(v, probs, TN) * my_live).astype(BF16)
        dh[h, 0] = dot(k, grads, TN).T
        dh[h, 1] = dot(grads, hq[h])
        dh[h, 2] = dot(probs, hg[h])
        return carry

    lax.fori_loop(0, HEADS, one_head, 0)
    ds[...] = jnp.concatenate(
        [dh[h, k] for k in range(3) for h in range(HEADS)]
        + [jnp.zeros((TV, PACK - 3 * GW), F32)],
        axis=1,
    ).astype(BF16)
    for d in range(1, NY):
        d_copy(d, True).start()
    d_own.start()

    for d in range(1, NY):
        x_copy(d, False).wait_recv()
    x_own.wait()

    def partial(cc):
        cols = pl.ds(pl.multiple_of(cc * HALF, HALF), HALF)
        return jnp.concatenate(
            [dot(ot[...], cr[:, cols]), dot(xr[...], cr[:, cols], TN)], axis=0
        )

    ws[...] = partial(1 - c).astype(BF16)
    k_copy = remote(ws, wr, k_ss, k_rs, core_peer)
    k_copy.start()
    own = partial(c)
    k_copy.wait_recv()
    wown[...] = (own + wr[...].astype(F32)).reshape(BLOCKS, NX, 8, HALF)

    for i in range(NX):
        x_s[i] = wown[:, i].reshape(BLOCKS * 8, HALF).astype(BF16)

    def xx_copy(d, mine):
        p = x_at(d)
        at = x if mine else p
        return remote(x_s.at[p], x_r.at[at], xx_ss.at[d], xx_rs.at[at], to_scene(z, p, c))

    for d in range(1, NX):
        xx_copy(d, True).start()
    total = wown[:, x].reshape(BLOCKS * 8, HALF)
    for d in range(1, NX):
        xx_copy(d, False).wait_recv()
        total = total + x_r[x_at(d)].astype(F32)
    zown[:BLOCKS] = total.reshape(BLOCKS, 8, HALF)
    for j in range(BLOCKS):
        zs[j] = total[8 * j : 8 * j + 8].astype(BF16)

    def local_block(zz):
        late = lax.div(zz, 6)
        return (1 - late) * zz + late * (6 + lax.rem(zz + 24 - 4 * group, 6))

    def z_copy(d, mine):
        p = z_at(d)
        at = z if mine else p
        return remote(zs.at[local_block(p)], zr.at[at], z_ss.at[d], z_rs.at[at], to_scene(p, x, c))

    for d in range(1, NZ):

        @pl.when(local_block(z_at(d)) < BLOCKS)
        def _():
            z_copy(d, True).start()

    late = lax.div(z, 6)
    mine_at = local_block(z)
    blk = (1 - late) * (6 * group + mine_at) + late * (18 + 4 * group + mine_at)
    owner = lax.div(blk, OWNED)
    y_copy = remote(yb, yr.at[view], y_ss, y_rs.at[view], to_y(owner))
    y_own = pltpu.make_async_copy(yb, yr.at[view], own_s.at[4])
    away = jnp.logical_and(mine_at < BLOCKS, owner != y)
    here = jnp.logical_and(mine_at < BLOCKS, owner == y)

    @pl.when(mine_at < BLOCKS)
    def _():
        acc = zown[mine_at]
        for d in range(1, NZ):
            z_copy(d, False).wait_recv()
            acc = acc + zr[z_at(d)].astype(F32)
        yb[...] = acc.astype(BF16)

    @pl.when(away)
    def _():
        y_copy.start()

    @pl.when(here)
    def _():
        y_own.start()

    tokens = TV * 2 * NZ * NX * 2
    slots = []
    for i in range(OWNED):
        b = y * OWNED + i
        high = lax.div(b, 24)
        rest = b - 24 * high
        src_group = (1 - high) * lax.div(rest, 6) + high * lax.div(rest, 4)
        src_z = 6 * high + lax.rem(b, 6)
        slots.append((src_group, src_z))

    def za_copy(i, d):
        piece = fc.at[c, x, i]
        return remote(piece, piece, za_ss.at[d], za_rs.at[i], to_scene(z_at(d), x, c))

    for i, (src_group, src_z) in enumerate(slots):

        @pl.when(src_z == z)
        def _():
            for v in range(2):
                src_y = v * GROUPS + src_group

                @pl.when(src_y != y)
                def _():
                    remote(yb, yr.at[v], y_ss, y_rs.at[v], to_y(src_y)).wait_recv()

                @pl.when(src_y == y)
                def _():
                    pltpu.make_async_copy(yb, yr.at[v], own_s.at[4]).wait()

            both = yr[0].astype(F32) + yr[1].astype(F32)
            fc[c, x, i] = (both * (1.0 / math.sqrt(tokens))).astype(BF16)
            for d in range(1, NZ):
                za_copy(i, d).start()

    for d in range(1, NY):
        d_copy(d, False).wait_recv()
    d_own.wait()
    trow = lax.broadcasted_iota(jnp.int32, (2 * POS, POS), 0)
    tcol = lax.broadcasted_iota(jnp.int32, (2 * POS, POS), 1)
    place = [jnp.where(trow == 2 * tcol + v, 1.0, 0.0).astype(BF16) for v in range(2)]
    for k in range(3):
        cols = slice(k * GW, (k + 1) * GW)
        acc = None
        for v in range(2):
            view_part = jnp.concatenate(
                [dr[v * GROUPS + g][:, cols].astype(F32) for g in range(GROUPS)], axis=1
            ).astype(BF16)
            full = jnp.concatenate([view_part, cg[k, v]], axis=1)
            t = dot(place[v], full)
            acc = t if acc is None else acc + t
        d_ref[k] = acc.astype(BF16)

    for i, (_, src_z) in enumerate(slots):

        @pl.when(src_z != z)
        def _():
            za_copy(i, 1).wait_recv()

    def xa_copy(d, mine):
        p = x_at(d)
        piece = fc.at[c, x if mine else p]
        return remote(piece, piece, xa_ss.at[d], xa_rs.at[x if mine else p], to_scene(z, p, c))

    for d in range(1, NX):
        xa_copy(d, True).start()
    for d in range(1, NX):
        xa_copy(d, False).wait_recv()
    ka_copy = remote(fc.at[c], fc.at[c], ka_ss, ka_rs, core_peer)
    ka_copy.start()
    remote(fc.at[1 - c], fc.at[1 - c], ka_ss, ka_rs, core_peer).wait_recv()
    for cc in range(2):
        for xx in range(NX):
            for i in range(OWNED):
                at = 32 * i + 8 * xx
                wg_ref[at : at + 8, cc * HALF : (cc + 1) * HALF] = fc[cc, xx, i].astype(F32)

    for d in range(1, NY):
        q_copy(d, True).wait_send()
        c_copy(d, True).wait_send()
        x_copy(d, True).wait_send()
        d_copy(d, True).wait_send()
    k_copy.wait_send()
    for d in range(1, NX):
        xx_copy(d, True).wait_send()
        xa_copy(d, True).wait_send()
    for d in range(1, NZ):

        @pl.when(local_block(z_at(d)) < BLOCKS)
        def _():
            z_copy(d, True).wait_send()

    @pl.when(away)
    def _():
        y_copy.wait_send()

    for i, (_, src_z) in enumerate(slots):

        @pl.when(src_z == z)
        def _():
            for d in range(1, NZ):
                za_copy(i, d).wait_send()

    ka_copy.wait_send()


def on_device(qkv, view_counts, out_weight, out_cotangent):
    vmem = pl.BlockSpec(memory_space=pltpu.VMEM)
    V = pltpu.VMEM
    S = pltpu.SemaphoreType.DMA
    return pl.pallas_call(
        kernel,
        out_shape=(
            jax.ShapeDtypeStruct((3, 2 * POS, WIDTH), BF16),
            jax.ShapeDtypeStruct((WIDTH // NY, WIDTH), F32),
        ),
        in_specs=[
            pl.BlockSpec(memory_space=pltpu.SMEM), vmem, vmem, pl.BlockSpec(memory_space=pl.ANY),
        ],
        out_specs=(vmem, vmem),
        scratch_shapes=[
            V((GW, WIDTH), BF16), V((CROSS_W, WIDTH), BF16),
            V((NY, POS, PACK), BF16), V((TV, PACK), BF16),
            V((2, POS, WIDTH), BF16), V((TV, WIDTH), BF16),
            V((3, 2, POS, CROSS_W), F32),
            V((NY, POS, 128), BF16), V((TV, 128), BF16),
            V((3, 2, POS, CROSS_W), BF16),
            V((HEADS, TV, HD), BF16), V((HEADS, TV, HD), BF16),
            V((HEADS, TV, HD), BF16), V((HEADS, TV, HD), BF16),
            V((TV, TV), BF16), V((TV, TV), BF16),
            V((HEADS, 3, TV, HD), F32),
            V((TV, PACK), BF16), V((NY, POS, PACK), BF16),
            V((GW, TV), BF16),
            V((320, HALF), BF16), V((320, HALF), BF16), V((BLOCKS, NX, 8, HALF), F32),
            V((NX, BLOCKS * 8, HALF), BF16), V((NX, BLOCKS * 8, HALF), BF16),
            V((NZ, 8, HALF), F32), V((NZ, 8, HALF), BF16), V((NZ, 8, HALF), BF16),
            V((8, HALF), BF16), V((2, 8, HALF), BF16), V((2, NX, OWNED, 8, HALF), BF16),
            S((2,)), S((NY,)), S((NY,)), S((NY,)), S((NY,)), S((NY,)), S((NY,)),
            S((NY,)), S((NY,)), S((5,)), S, S, S((NX,)), S((NX,)),
            S((NZ,)), S((NZ,)), S, S((2,)), S((NZ,)), S((OWNED,)), S((NX,)), S((NX,)), S, S,
        ],
        compiler_params=pltpu.CompilerParams(
            collective_id=0, has_side_effects=True, vmem_limit_bytes=60 * 1024 * 1024
        ),
        name="layer",
    )(view_counts, qkv, out_cotangent, out_weight)


def solution(mesh):
    in_specs = (P(None, ("scene", "seq"), None), P("scene"), P(), P(("scene", "seq"), None))
    out_specs = (P(None, ("scene", "seq"), None), P("seq", None))
    return jax.shard_map(
        on_device, mesh=mesh, in_specs=in_specs, out_specs=out_specs, check_vma=False
    )
```

```python
import functools
import math

import jax
import jax.numpy as jnp
from jax import lax
from jax.experimental import pallas as pl
from jax.experimental.pallas import tpu as pltpu
from jax.sharding import PartitionSpec as P

MESH = pl.DeviceIdType.MESH
F32 = jnp.float32
BF16 = jnp.bfloat16
NT = (((1,), (1,)), ((), ()))
TN = (((0,), (0,)), ((), ()))
NN = (((1,), (0,)), ((), ()))

HD = 64
NY, NX, NZ = 8, 4, 12
GROUPS = 4
HEADS = 3
POS = 64
TV = POS * NY
VIEW_W = 768
CROSS_W = 512
WIDTH = 1280
GW = HEADS * HD
PACK = 640
HALF = WIDTH // 2
BLOCKS = 10
OWNED = 5


def dot(a, b, dims=NN):
    return lax.dot_general(a, b, dims, preferred_element_type=F32)


def kernel(
    vc_ref, qkv_ref, cot_ref, w_ref, d_ref, wg_ref,
    wv, wc, qs, qr, cs, cr, cx, xs, xr, cg, hq, hk, hv, hg, pf, pr, dt, da, db, dc, ra, rb, rc, ot,
    ws, wr, wown, x_s, x_r, zown, zs, zr, yb, yr, fc,
    wsem, q_ss, q_rs, c_ss, c_rs, x_ss, x_rs, da_ss, da_rs, db_ss, db_rs, dc_ss, dc_rs, own_s, k_ss, k_rs, xx_ss, xx_rs,
    z_ss, z_rs, y_ss, y_rs, za_ss, za_rs, xa_ss, xa_rs, ka_ss, ka_rs,
):
    scene = lax.axis_index("scene")
    y = lax.axis_index("seq")
    c = lax.rem(scene, 2)
    x = lax.rem(lax.div(scene, 2), NX)
    z = lax.div(scene, 2 * NX)
    view = lax.div(y, GROUPS)
    group = lax.rem(y, GROUPS)

    def y_at(d):
        return lax.rem(y + d, NY)

    def z_at(d):
        return lax.rem(z + d, NZ)

    def x_at(d):
        return lax.rem(x + d, NX)

    def to_y(p):
        return {"seq": p}

    def to_scene(zz, xx, cc):
        return {"scene": (zz * NX + xx) * 2 + cc}

    core_peer = to_scene(z, x, 1 - c)

    def remote(src, dst, ssem, rsem, dev):
        return pltpu.make_async_remote_copy(
            src_ref=src, dst_ref=dst, send_sem=ssem, recv_sem=rsem, device_id=dev,
            device_id_type=MESH,
        )

    barrier = pltpu.get_barrier_semaphore()
    peers = [to_y(y_at(d)) for d in range(1, NY)]
    peers += [core_peer]
    peers += [to_scene(z, x_at(d), c) for d in range(1, NX)]
    peers += [to_scene(z_at(d), x, c) for d in range(1, NZ)]
    for peer in peers:
        pl.semaphore_signal(barrier, inc=1, device_id=peer, device_id_type=MESH)
    w_view = pltpu.make_async_copy(
        w_ref.at[pl.ds(pl.multiple_of(group * GW, GW), GW)], wv, wsem.at[0]
    )
    w_cross = pltpu.make_async_copy(w_ref.at[pl.ds(VIEW_W, CROSS_W)], wc, wsem.at[1])
    w_cross.start()
    w_view.start()

    vc = vc_ref[0]
    live = [jnp.where(vc > v, 1.0, 0.0).astype(F32) for v in range(2)]
    my_live = jnp.where(vc > view, 1.0, 0.0).astype(F32)

    row = lax.broadcasted_iota(jnp.int32, (POS, 2 * POS), 0)
    col = lax.broadcasted_iota(jnp.int32, (POS, 2 * POS), 1)
    for v in range(2):
        pick = jnp.where(col == 2 * row + v, 1.0, 0.0).astype(BF16)
        parts = []
        for k in range(3):
            r = dot(pick, qkv_ref[k])
            cx[k, v] = r[:, VIEW_W:]
            parts.append(r[:, :VIEW_W])
        for g in range(GROUPS):
            cols = slice(g * GW, (g + 1) * GW)
            packed = jnp.concatenate(
                [p[:, cols] for p in parts] + [jnp.zeros((POS, PACK - 3 * GW), F32)], axis=1
            )
            qs[v * GROUPS + g] = packed.astype(BF16)

    pl.semaphore_wait(barrier, len(peers))

    def rows_of(ref, p):
        return ref.at[pl.ds(pl.multiple_of(p * POS, POS), POS)]

    def q_copy(d, mine):
        p = y_at(d)
        at = y if mine else p
        return remote(qs.at[p], rows_of(qr, at), q_ss.at[d], q_rs.at[at], to_y(p))

    def c_copy(d, mine):
        p = y_at(d)
        at = y if mine else p
        return remote(
            cs.at[lax.div(p, GROUPS)], rows_of(cr, at), c_ss.at[d], c_rs.at[at], to_y(p)
        )

    def x_copy(d, mine):
        p = y_at(d)
        at = y if mine else p
        return remote(xs.at[p], rows_of(xr, at), x_ss.at[d], x_rs.at[at], to_y(p))

    returned = [(da, ra, da_ss, da_rs), (db, rb, db_ss, db_rs), (dc, rc, dc_ss, dc_rs)]

    def d_copy(n, d, mine):
        src, dst, ssem, rsem = returned[n]
        p = y_at(d)
        at = y if mine else p
        return remote(rows_of(src, p), dst.at[at], ssem.at[d], rsem.at[at], to_y(p))

    d_own = [
        pltpu.make_async_copy(rows_of(src, y), dst.at[y], own_s.at[5 + n])
        for n, (src, dst, _, _) in enumerate(returned)
    ]

    q_own = pltpu.make_async_copy(qs.at[y], rows_of(qr, y), own_s.at[0])
    c_own = pltpu.make_async_copy(cs.at[view], rows_of(cr, y), own_s.at[1])
    x_own = pltpu.make_async_copy(xs.at[y], rows_of(xr, y), own_s.at[2])

    for d in range(1, NY):
        q_copy(d, True).start()
    q_own.start()
    for v in range(2):
        pick = jnp.where(col == 2 * row + v, 1.0, 0.0).astype(BF16)
        cs[v] = dot(pick, cot_ref[...]).astype(BF16)
    for d in range(1, NY):
        c_copy(d, True).start()
    c_own.start()

    w_cross.wait()
    same = jnp.where(
        lax.broadcasted_iota(jnp.int32, (CROSS_W, CROSS_W), 0) // HD
        == lax.broadcasted_iota(jnp.int32, (CROSS_W, CROSS_W), 1) // HD,
        1.0,
        0.0,
    ).astype(BF16)

    def head_sum(t):
        hi = t.astype(BF16)
        lo = (t - hi.astype(F32)).astype(BF16)
        return dot(hi, same) + dot(lo, same)

    scale = 1.0 / math.sqrt(HD)
    gs = []
    for v in range(2):
        g = dot(cs[v], wc[...], NT).astype(BF16).astype(F32)
        gs.append(g * live[v])
    dq = []
    dk = [None, None]
    dv = [None, None]
    for a in range(2):
        q = cx[0, a]
        s0 = head_sum(q * cx[1, 0]) * scale
        s1 = head_sum(q * cx[1, 1]) * scale
        s1 = jnp.where(live[1] > 0.5, s1, -1e30)
        m = jnp.maximum(s0, s1)
        e0 = jnp.exp(s0 - m)
        e1 = jnp.exp(s1 - m)
        inv = 1.0 / (e0 + e1)
        p = [e0 * inv, e1 * inv]
        pb = [t.astype(BF16).astype(F32) for t in p]
        out = ((pb[0] * cx[2, 0] + pb[1] * cx[2, 1]) * live[a]).astype(BF16)
        for g in range(GROUPS):
            xs[a * GROUPS + g] = out[:, g * 128 : (g + 1) * 128]
        dp = [head_sum(gs[a] * cx[2, b]) for b in range(2)]
        mean = p[0] * dp[0] + p[1] * dp[1]
        grad = [p[b] * (dp[b] - mean) * scale for b in range(2)]
        dq.append(grad[0] * cx[1, 0] + grad[1] * cx[1, 1])
        for b in range(2):
            tk = grad[b] * q
            tv = pb[b] * gs[a]
            dk[b] = tk if dk[b] is None else dk[b] + tk
            dv[b] = tv if dv[b] is None else dv[b] + tv
    for d in range(1, NY):
        x_copy(d, True).start()
    x_own.start()
    for v in range(2):
        cg[0, v] = dq[v].astype(BF16)
        cg[1, v] = dk[v].astype(BF16)
        cg[2, v] = dv[v].astype(BF16)

    for d in range(1, NY):
        q_copy(d, False).wait_recv()
    q_own.wait()
    packed = qr[...]
    for h in range(HEADS):
        hq[h] = packed[:, h * HD : (h + 1) * HD]
        hk[h] = packed[:, GW + h * HD : GW + (h + 1) * HD]
        hv[h] = packed[:, 2 * GW + h * HD : 2 * GW + (h + 1) * HD]
    chunk = 128

    def forward(h, carry):
        k = hk[h]
        v = hv[h]
        for i in range(TV // chunk):
            at = slice(i * chunk, (i + 1) * chunk)
            s = dot(k, hq[h, at, :], NT) * scale
            e = jnp.exp(s - jnp.max(s, axis=0, keepdims=True))
            p = e * (1.0 / jnp.sum(e, axis=0, keepdims=True))
            pf[h, :, at] = p
            pr[h, :, at] = p.astype(BF16)
        ot[pl.ds(pl.multiple_of(h * HD, HD), HD), :] = (dot(v, pr[h], TN) * my_live).astype(BF16)
        return carry

    lax.fori_loop(0, HEADS, forward, 0)

    def backward(h):
        k = hk[h]
        v = hv[h]
        for i in range(TV // chunk):
            at = slice(i * chunk, (i + 1) * chunk)
            p = pf[h, :, at]
            dp = dot(v, hg[h, at, :], NT)
            mean = jnp.sum(p * dp, axis=0, keepdims=True)
            dt[:, at] = (p * (dp - mean) * scale).astype(BF16)
        grads = dt[...]
        return dot(k, grads, TN).T, dot(grads, hq[h]), dot(pr[h], hg[h])

    for d in range(1, NY):
        c_copy(d, False).wait_recv()
    c_own.wait()
    for d in range(1, NY):
        x_copy(d, False).wait_recv()
    x_own.wait()

    def partial(cc):
        cols = pl.ds(pl.multiple_of(cc * HALF, HALF), HALF)
        return jnp.concatenate(
            [dot(ot[...], cr[:, cols]), dot(xr[...], cr[:, cols], TN)], axis=0
        )

    ws[...] = partial(1 - c).astype(BF16)
    k_copy = remote(ws, wr, k_ss, k_rs, core_peer)
    k_copy.start()
    wown[...] = partial(c).reshape(BLOCKS, NX, 8, HALF)

    w_view.wait()
    g_all = (dot(cr[...], wv[...], NT).astype(BF16).astype(F32) * my_live).astype(BF16)
    for h in range(HEADS):
        hg[h] = g_all[:, h * HD : (h + 1) * HD]
    dq0, dk0, dv0 = backward(0)
    da[...] = jnp.concatenate([dq0, dk0], axis=1).astype(BF16)
    db[:, 2 * HD : 3 * HD] = dv0.astype(BF16)
    for d in range(1, NY):
        d_copy(0, d, True).start()
    d_own[0].start()

    k_copy.wait_recv()
    wown[...] = wown[...] + wr[...].astype(F32).reshape(BLOCKS, NX, 8, HALF)
    for i in range(NX):
        x_s[i] = wown[:, i].reshape(BLOCKS * 8, HALF).astype(BF16)

    def xx_copy(d, mine):
        p = x_at(d)
        at = x if mine else p
        return remote(x_s.at[p], x_r.at[at], xx_ss.at[d], xx_rs.at[at], to_scene(z, p, c))

    for d in range(1, NX):
        xx_copy(d, True).start()
    dq1, dk1, dv1 = backward(1)
    db[:, : 2 * HD] = jnp.concatenate([dq1, dk1], axis=1).astype(BF16)
    db[:, 3 * HD :] = dv1.astype(BF16)
    for d in range(1, NY):
        d_copy(1, d, True).start()
    d_own[1].start()
    total = wown[:, x].reshape(BLOCKS * 8, HALF)
    for d in range(1, NX):
        xx_copy(d, False).wait_recv()
        total = total + x_r[x_at(d)].astype(F32)
    zown[:BLOCKS] = total.reshape(BLOCKS, 8, HALF)
    for j in range(BLOCKS):
        zs[j] = total[8 * j : 8 * j + 8].astype(BF16)

    def local_block(zz):
        late = lax.div(zz, 6)
        return (1 - late) * zz + late * (6 + lax.rem(zz + 24 - 4 * group, 6))

    def z_copy(d, mine):
        p = z_at(d)
        at = z if mine else p
        return remote(zs.at[local_block(p)], zr.at[at], z_ss.at[d], z_rs.at[at], to_scene(p, x, c))

    for d in range(1, NZ):

        @pl.when(local_block(z_at(d)) < BLOCKS)
        def _():
            z_copy(d, True).start()

    dq2, dk2, dv2 = backward(2)
    dc[...] = jnp.concatenate([dq2, dk2, dv2, jnp.zeros((TV, HD), F32)], axis=1).astype(BF16)
    for d in range(1, NY):
        d_copy(2, d, True).start()
    d_own[2].start()

    late = lax.div(z, 6)
    mine_at = local_block(z)
    blk = (1 - late) * (6 * group + mine_at) + late * (18 + 4 * group + mine_at)
    owner = lax.div(blk, OWNED)
    y_copy = remote(yb, yr.at[view], y_ss, y_rs.at[view], to_y(owner))
    y_own = pltpu.make_async_copy(yb, yr.at[view], own_s.at[4])
    away = jnp.logical_and(mine_at < BLOCKS, owner != y)
    here = jnp.logical_and(mine_at < BLOCKS, owner == y)

    @pl.when(mine_at < BLOCKS)
    def _():
        acc = zown[mine_at]
        for d in range(1, NZ):
            z_copy(d, False).wait_recv()
            acc = acc + zr[z_at(d)].astype(F32)
        yb[...] = acc.astype(BF16)

    @pl.when(away)
    def _():
        y_copy.start()

    @pl.when(here)
    def _():
        y_own.start()

    tokens = TV * 2 * NZ * NX * 2
    slots = []
    for i in range(OWNED):
        b = y * OWNED + i
        high = lax.div(b, 24)
        rest = b - 24 * high
        src_group = (1 - high) * lax.div(rest, 6) + high * lax.div(rest, 4)
        src_z = 6 * high + lax.rem(b, 6)
        slots.append((src_group, src_z))

    def za_copy(i, d):
        piece = fc.at[c, x, i]
        return remote(piece, piece, za_ss.at[d], za_rs.at[i], to_scene(z_at(d), x, c))

    for i, (src_group, src_z) in enumerate(slots):

        @pl.when(src_z == z)
        def _():
            for v in range(2):
                src_y = v * GROUPS + src_group

                @pl.when(src_y != y)
                def _():
                    remote(yb, yr.at[v], y_ss, y_rs.at[v], to_y(src_y)).wait_recv()

                @pl.when(src_y == y)
                def _():
                    pltpu.make_async_copy(yb, yr.at[v], own_s.at[4]).wait()

            both = yr[0].astype(F32) + yr[1].astype(F32)
            fc[c, x, i] = (both * (1.0 / math.sqrt(tokens))).astype(BF16)
            for d in range(1, NZ):
                za_copy(i, d).start()

    for n in range(3):
        for d in range(1, NY):
            d_copy(n, d, False).wait_recv()
        d_own[n].wait()
    trow = lax.broadcasted_iota(jnp.int32, (2 * POS, POS), 0)
    tcol = lax.broadcasted_iota(jnp.int32, (2 * POS, POS), 1)
    place = [jnp.where(trow == 2 * tcol + v, 1.0, 0.0).astype(BF16) for v in range(2)]
    homes = [
        [(ra, 0), (rb, 0), (rc, 0)],
        [(ra, HD), (rb, HD), (rc, HD)],
        [(rb, 2 * HD), (rb, 3 * HD), (rc, 2 * HD)],
    ]
    for k in range(3):
        acc = None
        for v in range(2):
            view_part = jnp.concatenate(
                [
                    ref[v * GROUPS + g][:, lane : lane + HD].astype(F32)
                    for g in range(GROUPS)
                    for ref, lane in homes[k]
                ],
                axis=1,
            ).astype(BF16)
            full = jnp.concatenate([view_part, cg[k, v]], axis=1)
            t = dot(place[v], full)
            acc = t if acc is None else acc + t
        d_ref[k] = acc.astype(BF16)

    for i, (_, src_z) in enumerate(slots):

        @pl.when(src_z != z)
        def _():
            za_copy(i, 1).wait_recv()

    def xa_copy(d, mine):
        p = x_at(d)
        piece = fc.at[c, x if mine else p]
        return remote(piece, piece, xa_ss.at[d], xa_rs.at[x if mine else p], to_scene(z, p, c))

    for d in range(1, NX):
        xa_copy(d, True).start()
    for d in range(1, NX):
        xa_copy(d, False).wait_recv()
    ka_copy = remote(fc.at[c], fc.at[c], ka_ss, ka_rs, core_peer)
    ka_copy.start()
    remote(fc.at[1 - c], fc.at[1 - c], ka_ss, ka_rs, core_peer).wait_recv()
    for cc in range(2):
        for xx in range(NX):
            for i in range(OWNED):
                at = 32 * i + 8 * xx
                wg_ref[at : at + 8, cc * HALF : (cc + 1) * HALF] = fc[cc, xx, i].astype(F32)

    for d in range(1, NY):
        q_copy(d, True).wait_send()
        c_copy(d, True).wait_send()
        x_copy(d, True).wait_send()
        for n in range(3):
            d_copy(n, d, True).wait_send()
    k_copy.wait_send()
    for d in range(1, NX):
        xx_copy(d, True).wait_send()
        xa_copy(d, True).wait_send()
    for d in range(1, NZ):

        @pl.when(local_block(z_at(d)) < BLOCKS)
        def _():
            z_copy(d, True).wait_send()

    @pl.when(away)
    def _():
        y_copy.wait_send()

    for i, (_, src_z) in enumerate(slots):

        @pl.when(src_z == z)
        def _():
            for d in range(1, NZ):
                za_copy(i, d).wait_send()

    ka_copy.wait_send()


def on_device(qkv, view_counts, out_weight, out_cotangent):
    vmem = pl.BlockSpec(memory_space=pltpu.VMEM)
    V = pltpu.VMEM
    S = pltpu.SemaphoreType.DMA
    return pl.pallas_call(
        kernel,
        out_shape=(
            jax.ShapeDtypeStruct((3, 2 * POS, WIDTH), BF16),
            jax.ShapeDtypeStruct((WIDTH // NY, WIDTH), F32),
        ),
        in_specs=[
            pl.BlockSpec(memory_space=pltpu.SMEM), vmem, vmem, pl.BlockSpec(memory_space=pltpu.HBM),
        ],
        out_specs=(vmem, vmem),
        scratch_shapes=[
            V((GW, WIDTH), BF16), V((CROSS_W, WIDTH), BF16),
            V((NY, POS, PACK), BF16), V((TV, PACK), BF16),
            V((2, POS, WIDTH), BF16), V((TV, WIDTH), BF16),
            V((3, 2, POS, CROSS_W), F32),
            V((NY, POS, 128), BF16), V((TV, 128), BF16),
            V((3, 2, POS, CROSS_W), BF16),
            V((HEADS, TV, HD), BF16), V((HEADS, TV, HD), BF16),
            V((HEADS, TV, HD), BF16), V((HEADS, TV, HD), BF16),
            V((HEADS, TV, TV), F32), V((HEADS, TV, TV), BF16), V((TV, TV), BF16),
            V((TV, 128), BF16), V((TV, 256), BF16), V((TV, 256), BF16),
            V((NY, POS, 128), BF16), V((NY, POS, 256), BF16), V((NY, POS, 256), BF16),
            V((GW, TV), BF16),
            V((320, HALF), BF16), V((320, HALF), BF16), V((BLOCKS, NX, 8, HALF), F32),
            V((NX, BLOCKS * 8, HALF), BF16), V((NX, BLOCKS * 8, HALF), BF16),
            V((NZ, 8, HALF), F32), V((NZ, 8, HALF), BF16), V((NZ, 8, HALF), BF16),
            V((8, HALF), BF16), V((2, 8, HALF), BF16), V((2, NX, OWNED, 8, HALF), BF16),
            S((2,)), S((NY,)), S((NY,)), S((NY,)), S((NY,)), S((NY,)), S((NY,)),
            S((NY,)), S((NY,)), S((NY,)), S((NY,)), S((NY,)), S((NY,)), S((8,)), S, S, S((NX,)), S((NX,)),
            S((NZ,)), S((NZ,)), S, S((2,)), S((NZ,)), S((OWNED,)), S((NX,)), S((NX,)), S, S,
        ],
        compiler_params=pltpu.CompilerParams(
            collective_id=0, has_side_effects=True, vmem_limit_bytes=30 * 1024 * 1024
        ),
        name="layer",
    )(view_counts, qkv, out_cotangent, out_weight)


def solution(mesh):
    in_specs = (P(None, ("scene", "seq"), None), P("scene"), P(), P(("scene", "seq"), None))
    out_specs = (P(None, ("scene", "seq"), None), P("seq", None))
    return jax.shard_map(
        on_device, mesh=mesh, in_specs=in_specs, out_specs=out_specs, check_vma=False
    )
```

```python
import functools
import math

import jax
import jax.numpy as jnp
from jax import lax
from jax.experimental import pallas as pl
from jax.experimental.pallas import tpu as pltpu
from jax.sharding import PartitionSpec as P

MESH = pl.DeviceIdType.MESH
F32 = jnp.float32
BF16 = jnp.bfloat16
NT = (((1,), (1,)), ((), ()))
TN = (((0,), (0,)), ((), ()))
NN = (((1,), (0,)), ((), ()))

HD = 64
NY, NX, NZ = 8, 4, 12
GROUPS = 4
HEADS = 3
POS = 64
TV = POS * NY
VIEW_W = 768
CROSS_W = 512
WIDTH = 1280
GW = HEADS * HD
PACK = 640
HALF = WIDTH // 2
BLOCKS = 10
OWNED = 5


def dot(a, b, dims=NN):
    return lax.dot_general(a, b, dims, preferred_element_type=F32)


def kernel(
    vc_ref, qkv_hbm, cot_hbm, w_ref, d_ref, wg_ref,
    qkv_ref, cot_ref, rel,
    wv, wc, qs, qr, cs, cr, cx, xs, xr, cg, hq, hk, hv, hg, pf, pr, dt, da, db, dc, ra, rb, rc, ot,
    ws, wr, wown, x_s, x_r, zown, zs, zr, yb, yr, fc,
    wsem, q_ss, q_rs, c_lo, c_hi, c_out, c_rs, rel_rs, x_ss, x_rs, da_ss, da_rs, db_ss, db_rs, dc_ss, dc_rs, own_s, k_ss, k_rs, xx_ss, xx_rs,
    z_ss, z_rs, y_ss, y_rs, za_ss, za_rs, xa_ss, xa_rs, ka_ss, ka_rs,
):
    scene = lax.axis_index("scene")
    y = lax.axis_index("seq")
    c = lax.rem(scene, 2)
    x = lax.rem(lax.div(scene, 2), NX)
    z = lax.div(scene, 2 * NX)
    view = lax.div(y, GROUPS)
    group = lax.rem(y, GROUPS)

    def y_at(d):
        return lax.rem(y + d, NY)

    def z_at(d):
        return lax.rem(z + d, NZ)

    def x_at(d):
        return lax.rem(x + d, NX)

    def to_y(p):
        return {"seq": p}

    def to_scene(zz, xx, cc):
        return {"scene": (zz * NX + xx) * 2 + cc}

    core_peer = to_scene(z, x, 1 - c)

    def remote(src, dst, ssem, rsem, dev):
        return pltpu.make_async_remote_copy(
            src_ref=src, dst_ref=dst, send_sem=ssem, recv_sem=rsem, device_id=dev,
            device_id_type=MESH,
        )

    barrier = pltpu.get_barrier_semaphore()
    peers = [to_y(y_at(d)) for d in range(1, NY)]
    peers += [core_peer]
    peers += [to_scene(z, x_at(d), c) for d in range(1, NX)]
    peers += [to_scene(z_at(d), x, c) for d in range(1, NZ)]
    for peer in peers:
        pl.semaphore_signal(barrier, inc=1, device_id=peer, device_id_type=MESH)
    w_view = pltpu.make_async_copy(
        w_ref.at[pl.ds(pl.multiple_of(group * GW, GW), GW)], wv, wsem.at[0]
    )
    w_cross = pltpu.make_async_copy(w_ref.at[pl.ds(VIEW_W, CROSS_W)], wc, wsem.at[1])
    for k in range(3):
        pltpu.make_async_copy(qkv_hbm.at[k], qkv_ref.at[k], wsem.at[2 + k]).start()
    cot_in = pltpu.make_async_copy(cot_hbm, cot_ref, wsem.at[5])
    cot_in.start()
    w_cross.start()
    w_view.start()

    vc = vc_ref[0]
    live = [jnp.where(vc > v, 1.0, 0.0).astype(F32) for v in range(2)]
    my_live = jnp.where(vc > view, 1.0, 0.0).astype(F32)

    row = lax.broadcasted_iota(jnp.int32, (POS, 2 * POS), 0)
    col = lax.broadcasted_iota(jnp.int32, (POS, 2 * POS), 1)
    for k in range(3):
        pltpu.make_async_copy(qkv_hbm.at[k], qkv_ref.at[k], wsem.at[2 + k]).wait()
    for v in range(2):
        pick = jnp.where(col == 2 * row + v, 1.0, 0.0).astype(BF16)
        parts = []
        for k in range(3):
            r = dot(pick, qkv_ref[k])
            cx[k, v] = r[:, VIEW_W:]
            parts.append(r[:, :VIEW_W])
        for g in range(GROUPS):
            cols = slice(g * GW, (g + 1) * GW)
            packed = jnp.concatenate(
                [p[:, cols] for p in parts] + [jnp.zeros((POS, PACK - 3 * GW), F32)], axis=1
            )
            qs[v * GROUPS + g] = packed.astype(BF16)

    pl.semaphore_wait(barrier, len(peers))

    def rows_of(ref, p):
        return ref.at[pl.ds(pl.multiple_of(p * POS, POS), POS)]

    def q_copy(d, mine):
        p = y_at(d)
        at = y if mine else p
        return remote(qs.at[p], rows_of(qr, at), q_ss.at[d], q_rs.at[at], to_y(p))

    place_in = lax.rem(y, GROUPS)
    down, up = to_y(y_at(NY - 1)), to_y(y_at(1))

    def half_of(ref, p, h):
        return ref.at[pl.ds(pl.multiple_of(p * POS, POS), POS), pl.ds(h * HALF, HALF)]

    def sorted_rows(v, h):
        return cs.at[v, :, pl.ds(h * HALF, HALF)]

    def go_down(k, h):
        s = y_at(k)
        src = sorted_rows(view, h) if k == 0 else half_of(cr, s, h)
        return remote(src, half_of(cr, s, h), c_lo.at[h, k], c_rs.at[h, s], down)

    def go_up(k, h):
        s = y_at(NY - k)
        src = sorted_rows(view, h) if k == 0 else half_of(cr, s, h)
        return remote(src, half_of(cr, s, h), c_hi.at[h, k], c_rs.at[h, s], up)

    def arrives(s, h):
        return remote(half_of(cr, s, h), half_of(cr, s, h), c_lo.at[h, 0], c_rs.at[h, s], up)

    def enter(n, h):
        mine, relayed = sorted_rows(1 - view, h), rel.at[h]
        if n == 0:
            return remote(mine, half_of(cr, y, h), c_out.at[h, 0], c_rs.at[h, y], down)
        if n == 1:
            return remote(mine, relayed, c_out.at[h, 0], rel_rs.at[h], down)
        if n == 2:
            return remote(mine, relayed, c_out.at[h, 0], rel_rs.at[h], up)
        return remote(mine, half_of(cr, y, h), c_out.at[h, 0], c_rs.at[h, y], up)

    def relay(n, h):
        s, to = (y_at(1), down) if n == 0 else (y_at(NY - 1), up)
        return remote(rel.at[h], half_of(cr, s, h), c_out.at[h, 1], c_rs.at[h, s], to)

    def relay_in(h):
        return remote(rel.at[h], rel.at[h], c_out.at[h, 1], rel_rs.at[h], up)

    def cot_start(h):
        @pl.when(place_in >= 1)
        def _():
            go_down(0, h).start()

        @pl.when(place_in <= 2)
        def _():
            go_up(0, h).start()

        for n in range(GROUPS):

            @pl.when(place_in == n)
            def _():
                enter(n, h).start()

    def cot_flow(h):
        for n in (0, 3):

            @pl.when(place_in == n)
            def _():
                relay_in(h).wait_recv()
                relay(n, h).start()

        for k in range(1, 6):

            @pl.when(place_in <= 5 - k)
            def _():
                arrives(y_at(k), h).wait_recv()

                @pl.when(place_in >= 1)
                def _():
                    go_down(k, h).start()

            @pl.when(place_in >= k - 2)
            def _():
                arrives(y_at(NY - k), h).wait_recv()

                @pl.when(place_in <= 2)
                def _():
                    go_up(k, h).start()

    def cot_end(h):
        for n in range(GROUPS):

            @pl.when(place_in == n)
            def _():
                enter(n, h).wait_send()

        for n in (0, 3):

            @pl.when(place_in == n)
            def _():
                relay(n, h).wait_send()

        for k in range(6):

            @pl.when(jnp.logical_and(place_in <= 5 - k, place_in >= 1))
            def _():
                go_down(k, h).wait_send()

            @pl.when(jnp.logical_and(place_in >= k - 2, place_in <= 2))
            def _():
                go_up(k, h).wait_send()

    def x_copy(d, mine):
        p = y_at(d)
        at = y if mine else p
        return remote(xs.at[p], rows_of(xr, at), x_ss.at[d], x_rs.at[at], to_y(p))

    returned = [(da, ra, da_ss, da_rs), (db, rb, db_ss, db_rs), (dc, rc, dc_ss, dc_rs)]

    def d_copy(n, d, mine):
        src, dst, ssem, rsem = returned[n]
        p = y_at(d)
        at = y if mine else p
        return remote(rows_of(src, p), dst.at[at], ssem.at[d], rsem.at[at], to_y(p))

    d_own = [
        pltpu.make_async_copy(rows_of(src, y), dst.at[y], own_s.at[5 + n])
        for n, (src, dst, _, _) in enumerate(returned)
    ]

    q_own = pltpu.make_async_copy(qs.at[y], rows_of(qr, y), own_s.at[0])
    c_own = pltpu.make_async_copy(cs.at[view], rows_of(cr, y), own_s.at[1])
    x_own = pltpu.make_async_copy(xs.at[y], rows_of(xr, y), own_s.at[2])

    for d in range(1, NY):
        q_copy(d, True).start()
    q_own.start()
    cot_in.wait()
    for v in range(2):
        pick = jnp.where(col == 2 * row + v, 1.0, 0.0).astype(BF16)
        cs[v] = dot(pick, cot_ref[...]).astype(BF16)
    for h in range(2):
        cot_start(h)
    c_own.start()

    w_cross.wait()
    same = jnp.where(
        lax.broadcasted_iota(jnp.int32, (CROSS_W, CROSS_W), 0) // HD
        == lax.broadcasted_iota(jnp.int32, (CROSS_W, CROSS_W), 1) // HD,
        1.0,
        0.0,
    ).astype(BF16)

    def head_sum(t):
        hi = t.astype(BF16)
        lo = (t - hi.astype(F32)).astype(BF16)
        return dot(hi, same) + dot(lo, same)

    scale = 1.0 / math.sqrt(HD)
    gs = []
    for v in range(2):
        g = dot(cs[v], wc[...], NT).astype(BF16).astype(F32)
        gs.append(g * live[v])
    dq = []
    dk = [None, None]
    dv = [None, None]
    for a in range(2):
        q = cx[0, a]
        s0 = head_sum(q * cx[1, 0]) * scale
        s1 = head_sum(q * cx[1, 1]) * scale
        s1 = jnp.where(live[1] > 0.5, s1, -1e30)
        m = jnp.maximum(s0, s1)
        e0 = jnp.exp(s0 - m)
        e1 = jnp.exp(s1 - m)
        inv = 1.0 / (e0 + e1)
        p = [e0 * inv, e1 * inv]
        pb = [t.astype(BF16).astype(F32) for t in p]
        out = ((pb[0] * cx[2, 0] + pb[1] * cx[2, 1]) * live[a]).astype(BF16)
        for g in range(GROUPS):
            xs[a * GROUPS + g] = out[:, g * 128 : (g + 1) * 128]
        dp = [head_sum(gs[a] * cx[2, b]) for b in range(2)]
        mean = p[0] * dp[0] + p[1] * dp[1]
        grad = [p[b] * (dp[b] - mean) * scale for b in range(2)]
        dq.append(grad[0] * cx[1, 0] + grad[1] * cx[1, 1])
        for b in range(2):
            tk = grad[b] * q
            tv = pb[b] * gs[a]
            dk[b] = tk if dk[b] is None else dk[b] + tk
            dv[b] = tv if dv[b] is None else dv[b] + tv
    for d in range(1, NY):
        x_copy(d, True).start()
    x_own.start()
    for v in range(2):
        cg[0, v] = dq[v].astype(BF16)
        cg[1, v] = dk[v].astype(BF16)
        cg[2, v] = dv[v].astype(BF16)

    for d in range(1, NY):
        q_copy(d, False).wait_recv()
    q_own.wait()
    packed = qr[...]
    for h in range(HEADS):
        hq[h] = packed[:, h * HD : (h + 1) * HD]
        hk[h] = packed[:, GW + h * HD : GW + (h + 1) * HD]
        hv[h] = packed[:, 2 * GW + h * HD : 2 * GW + (h + 1) * HD]
    chunk = 128

    def forward(h, carry):
        k = hk[h]
        v = hv[h]
        for i in range(TV // chunk):
            at = slice(i * chunk, (i + 1) * chunk)
            s = dot(k, hq[h, at, :], NT) * scale
            e = jnp.exp(s - jnp.max(s, axis=0, keepdims=True))
            p = e * (1.0 / jnp.sum(e, axis=0, keepdims=True))
            pf[h, :, at] = p
            pr[h, :, at] = p.astype(BF16)
        ot[pl.ds(pl.multiple_of(h * HD, HD), HD), :] = (dot(v, pr[h], TN) * my_live).astype(BF16)
        return carry

    lax.fori_loop(0, HEADS, forward, 0)

    def backward(h):
        k = hk[h]
        v = hv[h]
        for i in range(TV // chunk):
            at = slice(i * chunk, (i + 1) * chunk)
            p = pf[h, :, at]
            dp = dot(v, hg[h, at, :], NT)
            mean = jnp.sum(p * dp, axis=0, keepdims=True)
            dt[:, at] = (p * (dp - mean) * scale).astype(BF16)
        grads = dt[...]
        return dot(k, grads, TN).T, dot(grads, hq[h]), dot(pr[h], hg[h])

    for h in range(2):
        cot_flow(h)
    c_own.wait()
    for d in range(1, NY):
        x_copy(d, False).wait_recv()
    x_own.wait()

    def partial(cc):
        cols = pl.ds(pl.multiple_of(cc * HALF, HALF), HALF)
        return jnp.concatenate(
            [dot(ot[...], cr[:, cols]), dot(xr[...], cr[:, cols], TN)], axis=0
        )

    ws[...] = partial(1 - c).astype(BF16)
    k_copy = remote(ws, wr, k_ss, k_rs, core_peer)
    k_copy.start()
    wown[...] = partial(c).reshape(BLOCKS, NX, 8, HALF)

    w_view.wait()
    g_all = (dot(cr[...], wv[...], NT).astype(BF16).astype(F32) * my_live).astype(BF16)
    for h in range(HEADS):
        hg[h] = g_all[:, h * HD : (h + 1) * HD]
    dq0, dk0, dv0 = backward(0)
    da[...] = jnp.concatenate([dq0, dk0], axis=1).astype(BF16)
    db[:, 2 * HD : 3 * HD] = dv0.astype(BF16)
    for d in range(1, NY):
        d_copy(0, d, True).start()
    d_own[0].start()

    k_copy.wait_recv()
    wown[...] = wown[...] + wr[...].astype(F32).reshape(BLOCKS, NX, 8, HALF)
    for i in range(NX):
        x_s[i] = wown[:, i].reshape(BLOCKS * 8, HALF).astype(BF16)

    def xx_copy(d, mine):
        p = x_at(d)
        at = x if mine else p
        return remote(x_s.at[p], x_r.at[at], xx_ss.at[d], xx_rs.at[at], to_scene(z, p, c))

    for d in range(1, NX):
        xx_copy(d, True).start()
    dq1, dk1, dv1 = backward(1)
    db[:, : 2 * HD] = jnp.concatenate([dq1, dk1], axis=1).astype(BF16)
    db[:, 3 * HD :] = dv1.astype(BF16)
    for d in range(1, NY):
        d_copy(1, d, True).start()
    d_own[1].start()
    total = wown[:, x].reshape(BLOCKS * 8, HALF)
    for d in range(1, NX):
        xx_copy(d, False).wait_recv()
        total = total + x_r[x_at(d)].astype(F32)
    zown[:BLOCKS] = total.reshape(BLOCKS, 8, HALF)
    for j in range(BLOCKS):
        zs[j] = total[8 * j : 8 * j + 8].astype(BF16)

    def local_block(zz):
        late = lax.div(zz, 6)
        return (1 - late) * zz + late * (6 + lax.rem(zz + 24 - 4 * group, 6))

    def z_copy(d, mine):
        p = z_at(d)
        at = z if mine else p
        return remote(zs.at[local_block(p)], zr.at[at], z_ss.at[d], z_rs.at[at], to_scene(p, x, c))

    for d in range(1, NZ):

        @pl.when(local_block(z_at(d)) < BLOCKS)
        def _():
            z_copy(d, True).start()

    dq2, dk2, dv2 = backward(2)
    dc[...] = jnp.concatenate([dq2, dk2, dv2, jnp.zeros((TV, HD), F32)], axis=1).astype(BF16)
    for d in range(1, NY):
        d_copy(2, d, True).start()
    d_own[2].start()

    late = lax.div(z, 6)
    mine_at = local_block(z)
    blk = (1 - late) * (6 * group + mine_at) + late * (18 + 4 * group + mine_at)
    owner = lax.div(blk, OWNED)
    y_copy = remote(yb, yr.at[view], y_ss, y_rs.at[view], to_y(owner))
    y_own = pltpu.make_async_copy(yb, yr.at[view], own_s.at[4])
    away = jnp.logical_and(mine_at < BLOCKS, owner != y)
    here = jnp.logical_and(mine_at < BLOCKS, owner == y)

    @pl.when(mine_at < BLOCKS)
    def _():
        acc = zown[mine_at]
        for d in range(1, NZ):
            z_copy(d, False).wait_recv()
            acc = acc + zr[z_at(d)].astype(F32)
        yb[...] = acc.astype(BF16)

    @pl.when(away)
    def _():
        y_copy.start()

    @pl.when(here)
    def _():
        y_own.start()

    tokens = TV * 2 * NZ * NX * 2
    slots = []
    for i in range(OWNED):
        b = y * OWNED + i
        high = lax.div(b, 24)
        rest = b - 24 * high
        src_group = (1 - high) * lax.div(rest, 6) + high * lax.div(rest, 4)
        src_z = 6 * high + lax.rem(b, 6)
        slots.append((src_group, src_z))

    def za_copy(i, d):
        piece = fc.at[c, x, i]
        return remote(piece, piece, za_ss.at[d], za_rs.at[i], to_scene(z_at(d), x, c))

    for i, (src_group, src_z) in enumerate(slots):

        @pl.when(src_z == z)
        def _():
            for v in range(2):
                src_y = v * GROUPS + src_group

                @pl.when(src_y != y)
                def _():
                    remote(yb, yr.at[v], y_ss, y_rs.at[v], to_y(src_y)).wait_recv()

                @pl.when(src_y == y)
                def _():
                    pltpu.make_async_copy(yb, yr.at[v], own_s.at[4]).wait()

            both = yr[0].astype(F32) + yr[1].astype(F32)
            fc[c, x, i] = (both * (1.0 / math.sqrt(tokens))).astype(BF16)
            for d in range(1, NZ):
                za_copy(i, d).start()

    for n in range(3):
        for d in range(1, NY):
            d_copy(n, d, False).wait_recv()
        d_own[n].wait()
    trow = lax.broadcasted_iota(jnp.int32, (2 * POS, POS), 0)
    tcol = lax.broadcasted_iota(jnp.int32, (2 * POS, POS), 1)
    place = [jnp.where(trow == 2 * tcol + v, 1.0, 0.0).astype(BF16) for v in range(2)]
    homes = [
        [(ra, 0), (rb, 0), (rc, 0)],
        [(ra, HD), (rb, HD), (rc, HD)],
        [(rb, 2 * HD), (rb, 3 * HD), (rc, 2 * HD)],
    ]
    for k in range(3):
        acc = None
        for v in range(2):
            view_part = jnp.concatenate(
                [
                    ref[v * GROUPS + g][:, lane : lane + HD].astype(F32)
                    for g in range(GROUPS)
                    for ref, lane in homes[k]
                ],
                axis=1,
            ).astype(BF16)
            full = jnp.concatenate([view_part, cg[k, v]], axis=1)
            t = dot(place[v], full)
            acc = t if acc is None else acc + t
        d_ref[k] = acc.astype(BF16)

    for i, (_, src_z) in enumerate(slots):

        @pl.when(src_z != z)
        def _():
            za_copy(i, 1).wait_recv()

    def xa_copy(d, mine):
        p = x_at(d)
        piece = fc.at[c, x if mine else p]
        return remote(piece, piece, xa_ss.at[d], xa_rs.at[x if mine else p], to_scene(z, p, c))

    for d in range(1, NX):
        xa_copy(d, True).start()
    for d in range(1, NX):
        xa_copy(d, False).wait_recv()
    ka_copy = remote(fc.at[c], fc.at[c], ka_ss, ka_rs, core_peer)
    ka_copy.start()
    remote(fc.at[1 - c], fc.at[1 - c], ka_ss, ka_rs, core_peer).wait_recv()
    for cc in range(2):
        for xx in range(NX):
            for i in range(OWNED):
                at = 32 * i + 8 * xx
                wg_ref[at : at + 8, cc * HALF : (cc + 1) * HALF] = fc[cc, xx, i].astype(F32)

    for h in range(2):
        cot_end(h)
    for d in range(1, NY):
        q_copy(d, True).wait_send()
        x_copy(d, True).wait_send()
        for n in range(3):
            d_copy(n, d, True).wait_send()
    k_copy.wait_send()
    for d in range(1, NX):
        xx_copy(d, True).wait_send()
        xa_copy(d, True).wait_send()
    for d in range(1, NZ):

        @pl.when(local_block(z_at(d)) < BLOCKS)
        def _():
            z_copy(d, True).wait_send()

    @pl.when(away)
    def _():
        y_copy.wait_send()

    for i, (_, src_z) in enumerate(slots):

        @pl.when(src_z == z)
        def _():
            for d in range(1, NZ):
                za_copy(i, d).wait_send()

    ka_copy.wait_send()


def on_device(qkv, view_counts, out_weight, out_cotangent):
    vmem = pl.BlockSpec(memory_space=pltpu.VMEM)
    hbm = pl.BlockSpec(memory_space=pltpu.HBM)
    V = pltpu.VMEM
    S = pltpu.SemaphoreType.DMA
    return pl.pallas_call(
        kernel,
        out_shape=(
            jax.ShapeDtypeStruct((3, 2 * POS, WIDTH), BF16),
            jax.ShapeDtypeStruct((WIDTH // NY, WIDTH), F32),
        ),
        in_specs=[
            pl.BlockSpec(memory_space=pltpu.SMEM), hbm, hbm, hbm,
        ],
        out_specs=(vmem, vmem),
        scratch_shapes=[
            V((3, 2 * POS, WIDTH), BF16), V((2 * POS, WIDTH), BF16), V((2, POS, HALF), BF16),
            V((GW, WIDTH), BF16), V((CROSS_W, WIDTH), BF16),
            V((NY, POS, PACK), BF16), V((TV, PACK), BF16),
            V((2, POS, WIDTH), BF16), V((TV, WIDTH), BF16),
            V((3, 2, POS, CROSS_W), F32),
            V((NY, POS, 128), BF16), V((TV, 128), BF16),
            V((3, 2, POS, CROSS_W), BF16),
            V((HEADS, TV, HD), BF16), V((HEADS, TV, HD), BF16),
            V((HEADS, TV, HD), BF16), V((HEADS, TV, HD), BF16),
            V((HEADS, TV, TV), F32), V((HEADS, TV, TV), BF16), V((TV, TV), BF16),
            V((TV, 128), BF16), V((TV, 256), BF16), V((TV, 256), BF16),
            V((NY, POS, 128), BF16), V((NY, POS, 256), BF16), V((NY, POS, 256), BF16),
            V((GW, TV), BF16),
            V((320, HALF), BF16), V((320, HALF), BF16), V((BLOCKS, NX, 8, HALF), F32),
            V((NX, BLOCKS * 8, HALF), BF16), V((NX, BLOCKS * 8, HALF), BF16),
            V((NZ, 8, HALF), F32), V((NZ, 8, HALF), BF16), V((NZ, 8, HALF), BF16),
            V((8, HALF), BF16), V((2, 8, HALF), BF16), V((2, NX, OWNED, 8, HALF), BF16),
            S((6,)), S((NY,)), S((NY,)),
            S((2, 6)), S((2, 6)), S((2, 2)), S((2, NY)), S((2,)),
            S((NY,)), S((NY,)),
            S((NY,)), S((NY,)), S((NY,)), S((NY,)), S((NY,)), S((NY,)), S((8,)), S, S, S((NX,)), S((NX,)),
            S((NZ,)), S((NZ,)), S, S((2,)), S((NZ,)), S((OWNED,)), S((NX,)), S((NX,)), S, S,
        ],
        compiler_params=pltpu.CompilerParams(
            collective_id=0, has_side_effects=True, vmem_limit_bytes=30 * 1024 * 1024
        ),
        name="layer",
    )(view_counts, *(pltpu.with_memory_space_constraint(a, pltpu.HBM) for a in (qkv, out_cotangent, out_weight)))


def solution(mesh):
    in_specs = (P(None, ("scene", "seq"), None), P("scene"), P(), P(("scene", "seq"), None))
    out_specs = (P(None, ("scene", "seq"), None), P("seq", None))
    return jax.shard_map(
        on_device, mesh=mesh, in_specs=in_specs, out_specs=out_specs, check_vma=False
    )
```

```python
import functools
import math

import jax
import jax.numpy as jnp
from jax import lax
from jax.experimental import pallas as pl
from jax.experimental.pallas import tpu as pltpu
from jax.sharding import PartitionSpec as P

MESH = pl.DeviceIdType.MESH
F32 = jnp.float32
BF16 = jnp.bfloat16
NT = (((1,), (1,)), ((), ()))
TN = (((0,), (0,)), ((), ()))
NN = (((1,), (0,)), ((), ()))

HD = 64
NY, NX, NZ = 8, 4, 12
GROUPS = 4
HEADS = 3
POS = 64
TV = POS * NY
VIEW_W = 768
CROSS_W = 512
WIDTH = 1280
GW = HEADS * HD
PACK = 640
HALF = WIDTH // 2
BLOCKS = 10
OWNED = 5


def dot(a, b, dims=NN):
    return lax.dot_general(a, b, dims, preferred_element_type=F32)


def kernel(
    vc_ref, qkv_hbm, cot_hbm, w_ref, d_ref, wg_ref,
    qkv_ref, cot_ref, rel,
    wv, wc, qs, qr, cs, cr, cx, xs, xr, cg, hq, hk, hv, hg, pf, pr, dt, da, db, dc, ra, rb, rc, ot,
    ws, wr, wown, x_s, x_r, zown, zs, zr, yb, yr, fc,
    wsem, q_ss, q_rs, c_lo, c_hi, c_out, c_rs, rel_rs, x_ss, x_rs, da_ss, da_rs, db_ss, db_rs, dc_ss, dc_rs, own_s, k_ss, k_rs, xx_ss, xx_rs,
    z_ss, z_rs, y_ss, y_rs, za_ss, za_rs, xa_ss, xa_rs, ka_ss, ka_rs,
):
    scene = lax.axis_index("scene")
    y = lax.axis_index("seq")
    c = lax.rem(scene, 2)
    x = lax.rem(lax.div(scene, 2), NX)
    z = lax.div(scene, 2 * NX)
    view = lax.div(y, GROUPS)
    group = lax.rem(y, GROUPS)

    def y_at(d):
        return lax.rem(y + d, NY)

    def z_at(d):
        return lax.rem(z + d, NZ)

    def x_at(d):
        return lax.rem(x + d, NX)

    def to_y(p):
        return {"seq": p}

    def to_scene(zz, xx, cc):
        return {"scene": (zz * NX + xx) * 2 + cc}

    core_peer = to_scene(z, x, 1 - c)

    def remote(src, dst, ssem, rsem, dev):
        return pltpu.make_async_remote_copy(
            src_ref=src, dst_ref=dst, send_sem=ssem, recv_sem=rsem, device_id=dev,
            device_id_type=MESH,
        )

    barrier = pltpu.get_barrier_semaphore()
    peers = [to_y(y_at(d)) for d in range(1, NY)]
    peers += [core_peer]
    peers += [to_scene(z, x_at(d), c) for d in range(1, NX)]
    peers += [to_scene(z_at(d), x, c) for d in range(1, NZ)]
    for peer in peers:
        pl.semaphore_signal(barrier, inc=1, device_id=peer, device_id_type=MESH)
    w_view = pltpu.make_async_copy(
        w_ref.at[pl.ds(pl.multiple_of(group * GW, GW), GW)], wv, wsem.at[0]
    )
    w_cross = pltpu.make_async_copy(w_ref.at[pl.ds(VIEW_W, CROSS_W)], wc, wsem.at[1])
    for k in range(3):
        pltpu.make_async_copy(qkv_hbm.at[k], qkv_ref.at[k], wsem.at[2 + k]).start()
    cot_in = pltpu.make_async_copy(cot_hbm, cot_ref, wsem.at[5])
    cot_in.start()
    w_cross.start()
    w_view.start()

    vc = vc_ref[0]
    live = [jnp.where(vc > v, 1.0, 0.0).astype(F32) for v in range(2)]
    my_live = jnp.where(vc > view, 1.0, 0.0).astype(F32)

    def rows_of(ref, p):
        return ref.at[pl.ds(pl.multiple_of(p * POS, POS), POS)]

    def q_send(p):
        return remote(qs.at[p], rows_of(qr, y), q_ss.at[p], q_rs.at[y], to_y(p))

    def q_arrives(p):
        return remote(rows_of(qr, p), rows_of(qr, p), q_ss.at[0], q_rs.at[p], to_y(p))

    row = lax.broadcasted_iota(jnp.int32, (POS, 2 * POS), 0)
    col = lax.broadcasted_iota(jnp.int32, (POS, 2 * POS), 1)
    for k in range(3):
        pltpu.make_async_copy(qkv_hbm.at[k], qkv_ref.at[k], wsem.at[2 + k]).wait()
    for v in range(2):
        pick = jnp.where(col == 2 * row + v, 1.0, 0.0).astype(BF16)
        parts = []
        for k in range(3):
            parts.append(dot(pick, qkv_ref[k, :, :VIEW_W]))
        for g in range(GROUPS):
            cols = slice(g * GW, (g + 1) * GW)
            packed = jnp.concatenate(
                [p[:, cols] for p in parts] + [jnp.zeros((POS, PACK - 3 * GW), F32)], axis=1
            )
            qs[v * GROUPS + g] = packed.astype(BF16)
        if v == 0:
            pl.semaphore_wait(barrier, len(peers))
        for p in range(v * GROUPS, (v + 1) * GROUPS):

            @pl.when(p != y)
            def _():
                q_send(p).start()


    place_in = lax.rem(y, GROUPS)
    down, up = to_y(y_at(NY - 1)), to_y(y_at(1))

    def half_of(ref, p, h):
        return ref.at[pl.ds(pl.multiple_of(p * POS, POS), POS), pl.ds(h * HALF, HALF)]

    def sorted_rows(v, h):
        return cs.at[v, :, pl.ds(h * HALF, HALF)]

    def go_down(k, h):
        s = y_at(k)
        src = sorted_rows(view, h) if k == 0 else half_of(cr, s, h)
        return remote(src, half_of(cr, s, h), c_lo.at[h, k], c_rs.at[h, s], down)

    def go_up(k, h):
        s = y_at(NY - k)
        src = sorted_rows(view, h) if k == 0 else half_of(cr, s, h)
        return remote(src, half_of(cr, s, h), c_hi.at[h, k], c_rs.at[h, s], up)

    def arrives(s, h):
        return remote(half_of(cr, s, h), half_of(cr, s, h), c_lo.at[h, 0], c_rs.at[h, s], up)

    def enter(n, h):
        mine, relayed = sorted_rows(1 - view, h), rel.at[h]
        if n == 0:
            return remote(mine, half_of(cr, y, h), c_out.at[h, 0], c_rs.at[h, y], down)
        if n == 1:
            return remote(mine, relayed, c_out.at[h, 0], rel_rs.at[h], down)
        if n == 2:
            return remote(mine, relayed, c_out.at[h, 0], rel_rs.at[h], up)
        return remote(mine, half_of(cr, y, h), c_out.at[h, 0], c_rs.at[h, y], up)

    def relay(n, h):
        s, to = (y_at(1), down) if n == 0 else (y_at(NY - 1), up)
        return remote(rel.at[h], half_of(cr, s, h), c_out.at[h, 1], c_rs.at[h, s], to)

    def relay_in(h):
        return remote(rel.at[h], rel.at[h], c_out.at[h, 1], rel_rs.at[h], up)

    def cot_start(h):
        @pl.when(place_in >= 1)
        def _():
            go_down(0, h).start()

        @pl.when(place_in <= 2)
        def _():
            go_up(0, h).start()

        for n in range(GROUPS):

            @pl.when(place_in == n)
            def _():
                enter(n, h).start()

    def cot_flow():
        for n in (0, 3):

            @pl.when(place_in == n)
            def _():
                for h in range(2):
                    relay_in(h).wait_recv()
                    relay(n, h).start()

        for k in range(1, 6):
            for h in range(2):

                @pl.when(place_in <= 5 - k)
                def _():
                    arrives(y_at(k), h).wait_recv()

                    @pl.when(place_in >= 1)
                    def _():
                        go_down(k, h).start()

                @pl.when(place_in >= k - 2)
                def _():
                    arrives(y_at(NY - k), h).wait_recv()

                    @pl.when(place_in <= 2)
                    def _():
                        go_up(k, h).start()

    def cot_end(h):
        for n in range(GROUPS):

            @pl.when(place_in == n)
            def _():
                enter(n, h).wait_send()

        for n in (0, 3):

            @pl.when(place_in == n)
            def _():
                relay(n, h).wait_send()

        for k in range(6):

            @pl.when(jnp.logical_and(place_in <= 5 - k, place_in >= 1))
            def _():
                go_down(k, h).wait_send()

            @pl.when(jnp.logical_and(place_in >= k - 2, place_in <= 2))
            def _():
                go_up(k, h).wait_send()

    def x_copy(d, mine):
        p = y_at(d)
        at = y if mine else p
        return remote(xs.at[p], rows_of(xr, at), x_ss.at[d], x_rs.at[at], to_y(p))

    returned = [(da, ra, da_ss, da_rs), (db, rb, db_ss, db_rs), (dc, rc, dc_ss, dc_rs)]

    def d_copy(n, d, mine):
        src, dst, ssem, rsem = returned[n]
        p = y_at(d)
        at = y if mine else p
        return remote(rows_of(src, p), dst.at[at], ssem.at[d], rsem.at[at], to_y(p))

    d_own = [
        pltpu.make_async_copy(rows_of(src, y), dst.at[y], own_s.at[5 + n])
        for n, (src, dst, _, _) in enumerate(returned)
    ]

    q_own = pltpu.make_async_copy(qs.at[y], rows_of(qr, y), own_s.at[0])
    c_own = pltpu.make_async_copy(cs.at[view], rows_of(cr, y), own_s.at[1])
    x_own = pltpu.make_async_copy(xs.at[y], rows_of(xr, y), own_s.at[2])

    q_own.start()
    cot_in.wait()
    for v in range(2):
        pick = jnp.where(col == 2 * row + v, 1.0, 0.0).astype(BF16)
        cs[v] = dot(pick, cot_ref[...]).astype(BF16)
    for h in range(2):
        cot_start(h)
    c_own.start()
    for v in range(2):
        pick = jnp.where(col == 2 * row + v, 1.0, 0.0).astype(BF16)
        for k in range(3):
            cx[k, v] = dot(pick, qkv_ref[k, :, VIEW_W:])

    w_cross.wait()
    same = jnp.where(
        lax.broadcasted_iota(jnp.int32, (CROSS_W, CROSS_W), 0) // HD
        == lax.broadcasted_iota(jnp.int32, (CROSS_W, CROSS_W), 1) // HD,
        1.0,
        0.0,
    ).astype(BF16)

    def head_sum(t):
        hi = t.astype(BF16)
        lo = (t - hi.astype(F32)).astype(BF16)
        return dot(hi, same) + dot(lo, same)

    scale = 1.0 / math.sqrt(HD)
    gs = []
    for v in range(2):
        g = dot(cs[v], wc[...], NT).astype(BF16).astype(F32)
        gs.append(g * live[v])
    dq = []
    dk = [None, None]
    dv = [None, None]
    for a in range(2):
        q = cx[0, a]
        s0 = head_sum(q * cx[1, 0]) * scale
        s1 = head_sum(q * cx[1, 1]) * scale
        s1 = jnp.where(live[1] > 0.5, s1, -1e30)
        m = jnp.maximum(s0, s1)
        e0 = jnp.exp(s0 - m)
        e1 = jnp.exp(s1 - m)
        inv = 1.0 / (e0 + e1)
        p = [e0 * inv, e1 * inv]
        pb = [t.astype(BF16).astype(F32) for t in p]
        out = ((pb[0] * cx[2, 0] + pb[1] * cx[2, 1]) * live[a]).astype(BF16)
        for g in range(GROUPS):
            xs[a * GROUPS + g] = out[:, g * 128 : (g + 1) * 128]
        dp = [head_sum(gs[a] * cx[2, b]) for b in range(2)]
        mean = p[0] * dp[0] + p[1] * dp[1]
        grad = [p[b] * (dp[b] - mean) * scale for b in range(2)]
        dq.append(grad[0] * cx[1, 0] + grad[1] * cx[1, 1])
        for b in range(2):
            tk = grad[b] * q
            tv = pb[b] * gs[a]
            dk[b] = tk if dk[b] is None else dk[b] + tk
            dv[b] = tv if dv[b] is None else dv[b] + tv
    for d in range(1, NY):
        x_copy(d, True).start()
    x_own.start()
    for v in range(2):
        cg[0, v] = dq[v].astype(BF16)
        cg[1, v] = dk[v].astype(BF16)
        cg[2, v] = dv[v].astype(BF16)

    for d in range(1, NY):
        q_arrives(y_at(d)).wait_recv()
    q_own.wait()
    packed = qr[...]
    for h in range(HEADS):
        hq[h] = packed[:, h * HD : (h + 1) * HD]
        hk[h] = packed[:, GW + h * HD : GW + (h + 1) * HD]
        hv[h] = packed[:, 2 * GW + h * HD : 2 * GW + (h + 1) * HD]
    chunk = 128

    def forward(h, carry):
        k = hk[h]
        v = hv[h]
        for i in range(TV // chunk):
            at = slice(i * chunk, (i + 1) * chunk)
            s = dot(k, hq[h, at, :], NT) * scale
            e = jnp.exp(s - jnp.max(s, axis=0, keepdims=True))
            p = e * (1.0 / jnp.sum(e, axis=0, keepdims=True))
            pf[h, :, at] = p
            pr[h, :, at] = p.astype(BF16)
        ot[pl.ds(pl.multiple_of(h * HD, HD), HD), :] = (dot(v, pr[h], TN) * my_live).astype(BF16)
        return carry

    lax.fori_loop(0, HEADS, forward, 0)

    def backward(h):
        k = hk[h]
        v = hv[h]
        for i in range(TV // chunk):
            at = slice(i * chunk, (i + 1) * chunk)
            p = pf[h, :, at]
            dp = dot(v, hg[h, at, :], NT)
            mean = jnp.sum(p * dp, axis=0, keepdims=True)
            dt[:, at] = (p * (dp - mean) * scale).astype(BF16)
        grads = dt[...]
        return dot(k, grads, TN).T, dot(grads, hq[h]), dot(pr[h], hg[h])

    cot_flow()
    c_own.wait()
    for d in range(1, NY):
        x_copy(d, False).wait_recv()
    x_own.wait()

    def partial(cc):
        cols = pl.ds(pl.multiple_of(cc * HALF, HALF), HALF)
        return jnp.concatenate(
            [dot(ot[...], cr[:, cols]), dot(xr[...], cr[:, cols], TN)], axis=0
        )

    ws[...] = partial(1 - c).astype(BF16)
    k_copy = remote(ws, wr, k_ss, k_rs, core_peer)
    k_copy.start()
    wown[...] = partial(c).reshape(BLOCKS, NX, 8, HALF)

    w_view.wait()
    g_all = (dot(cr[...], wv[...], NT).astype(BF16).astype(F32) * my_live).astype(BF16)
    for h in range(HEADS):
        hg[h] = g_all[:, h * HD : (h + 1) * HD]
    dq0, dk0, dv0 = backward(0)
    da[...] = jnp.concatenate([dq0, dk0], axis=1).astype(BF16)
    db[:, 2 * HD : 3 * HD] = dv0.astype(BF16)
    for d in range(1, NY):
        d_copy(0, d, True).start()
    d_own[0].start()

    k_copy.wait_recv()
    wown[...] = wown[...] + wr[...].astype(F32).reshape(BLOCKS, NX, 8, HALF)
    for i in range(NX):
        x_s[i] = wown[:, i].reshape(BLOCKS * 8, HALF).astype(BF16)

    def xx_copy(d, mine):
        p = x_at(d)
        at = x if mine else p
        return remote(x_s.at[p], x_r.at[at], xx_ss.at[d], xx_rs.at[at], to_scene(z, p, c))

    for d in range(1, NX):
        xx_copy(d, True).start()
    dq1, dk1, dv1 = backward(1)
    db[:, : 2 * HD] = jnp.concatenate([dq1, dk1], axis=1).astype(BF16)
    db[:, 3 * HD :] = dv1.astype(BF16)
    for d in range(1, NY):
        d_copy(1, d, True).start()
    d_own[1].start()
    total = wown[:, x].reshape(BLOCKS * 8, HALF)
    for d in range(1, NX):
        xx_copy(d, False).wait_recv()
        total = total + x_r[x_at(d)].astype(F32)
    zown[:BLOCKS] = total.reshape(BLOCKS, 8, HALF)
    for j in range(BLOCKS):
        zs[j] = total[8 * j : 8 * j + 8].astype(BF16)

    def local_block(zz):
        late = lax.div(zz, 6)
        return (1 - late) * zz + late * (6 + lax.rem(zz + 24 - 4 * group, 6))

    def z_copy(d, mine):
        p = z_at(d)
        at = z if mine else p
        return remote(zs.at[local_block(p)], zr.at[at], z_ss.at[d], z_rs.at[at], to_scene(p, x, c))

    for d in range(1, NZ):

        @pl.when(local_block(z_at(d)) < BLOCKS)
        def _():
            z_copy(d, True).start()

    dq2, dk2, dv2 = backward(2)
    dc[...] = jnp.concatenate([dq2, dk2, dv2, jnp.zeros((TV, HD), F32)], axis=1).astype(BF16)
    late = lax.div(z, 6)
    mine_at = local_block(z)
    blk = (1 - late) * (6 * group + mine_at) + late * (18 + 4 * group + mine_at)
    owner = lax.div(blk, OWNED)
    y_copy = remote(yb, yr.at[view], y_ss, y_rs.at[view], to_y(owner))
    y_own = pltpu.make_async_copy(yb, yr.at[view], own_s.at[4])
    away = jnp.logical_and(mine_at < BLOCKS, owner != y)
    here = jnp.logical_and(mine_at < BLOCKS, owner == y)

    @pl.when(mine_at < BLOCKS)
    def _():
        acc = zown[mine_at]
        for d in range(1, NZ):
            z_copy(d, False).wait_recv()
            acc = acc + zr[z_at(d)].astype(F32)
        yb[...] = acc.astype(BF16)

    @pl.when(away)
    def _():
        y_copy.start()

    @pl.when(here)
    def _():
        y_own.start()

    for d in range(1, NY):
        d_copy(2, d, True).start()
    d_own[2].start()

    tokens = TV * 2 * NZ * NX * 2
    slots = []
    for i in range(OWNED):
        b = y * OWNED + i
        high = lax.div(b, 24)
        rest = b - 24 * high
        src_group = (1 - high) * lax.div(rest, 6) + high * lax.div(rest, 4)
        src_z = 6 * high + lax.rem(b, 6)
        slots.append((src_group, src_z))

    def za_copy(i, d):
        piece = fc.at[c, x, i]
        return remote(piece, piece, za_ss.at[d], za_rs.at[i], to_scene(z_at(d), x, c))

    for i, (src_group, src_z) in enumerate(slots):

        @pl.when(src_z == z)
        def _():
            for v in range(2):
                src_y = v * GROUPS + src_group

                @pl.when(src_y != y)
                def _():
                    remote(yb, yr.at[v], y_ss, y_rs.at[v], to_y(src_y)).wait_recv()

                @pl.when(src_y == y)
                def _():
                    pltpu.make_async_copy(yb, yr.at[v], own_s.at[4]).wait()

            both = yr[0].astype(F32) + yr[1].astype(F32)
            fc[c, x, i] = (both * (1.0 / math.sqrt(tokens))).astype(BF16)
            for d in range(1, NZ):
                za_copy(i, d).start()

    for n in range(3):
        for d in range(1, NY):
            d_copy(n, d, False).wait_recv()
        d_own[n].wait()
    trow = lax.broadcasted_iota(jnp.int32, (2 * POS, POS), 0)
    tcol = lax.broadcasted_iota(jnp.int32, (2 * POS, POS), 1)
    place = [jnp.where(trow == 2 * tcol + v, 1.0, 0.0).astype(BF16) for v in range(2)]
    homes = [
        [(ra, 0), (rb, 0), (rc, 0)],
        [(ra, HD), (rb, HD), (rc, HD)],
        [(rb, 2 * HD), (rb, 3 * HD), (rc, 2 * HD)],
    ]
    for k in range(3):
        acc = None
        for v in range(2):
            view_part = jnp.concatenate(
                [
                    ref[v * GROUPS + g][:, lane : lane + HD].astype(F32)
                    for g in range(GROUPS)
                    for ref, lane in homes[k]
                ],
                axis=1,
            ).astype(BF16)
            full = jnp.concatenate([view_part, cg[k, v]], axis=1)
            t = dot(place[v], full)
            acc = t if acc is None else acc + t
        d_ref[k] = acc.astype(BF16)

    for i, (_, src_z) in enumerate(slots):

        @pl.when(src_z != z)
        def _():
            za_copy(i, 1).wait_recv()

    def xa_copy(d, mine):
        p = x_at(d)
        piece = fc.at[c, x if mine else p]
        return remote(piece, piece, xa_ss.at[d], xa_rs.at[x if mine else p], to_scene(z, p, c))

    def ka_copy(cc, xx):
        return remote(fc.at[cc, xx], fc.at[cc, xx], ka_ss.at[xx], ka_rs.at[xx], core_peer)

    for d in range(1, NX):
        xa_copy(d, True).start()
    ka_copy(c, x).start()
    for d in (1, 3, 2):
        xa_copy(d, False).wait_recv()
        ka_copy(c, x_at(d)).start()
    for xx in range(NX):
        ka_copy(1 - c, xx).wait_recv()
    for cc in range(2):
        for xx in range(NX):
            for i in range(OWNED):
                at = 32 * i + 8 * xx
                wg_ref[at : at + 8, cc * HALF : (cc + 1) * HALF] = fc[cc, xx, i].astype(F32)

    for p in range(NY):

        @pl.when(p != y)
        def _():
            q_send(p).wait_send()

    for h in range(2):
        cot_end(h)
    for d in range(1, NY):
        x_copy(d, True).wait_send()
        for n in range(3):
            d_copy(n, d, True).wait_send()
    k_copy.wait_send()
    for d in range(1, NX):
        xx_copy(d, True).wait_send()
        xa_copy(d, True).wait_send()
    for d in range(1, NZ):

        @pl.when(local_block(z_at(d)) < BLOCKS)
        def _():
            z_copy(d, True).wait_send()

    @pl.when(away)
    def _():
        y_copy.wait_send()

    for i, (_, src_z) in enumerate(slots):

        @pl.when(src_z == z)
        def _():
            for d in range(1, NZ):
                za_copy(i, d).wait_send()

    for xx in range(NX):
        ka_copy(c, xx).wait_send()


def on_device(qkv, view_counts, out_weight, out_cotangent):
    vmem = pl.BlockSpec(memory_space=pltpu.VMEM)
    hbm = pl.BlockSpec(memory_space=pltpu.HBM)
    V = pltpu.VMEM
    S = pltpu.SemaphoreType.DMA
    return pl.pallas_call(
        kernel,
        out_shape=(
            jax.ShapeDtypeStruct((3, 2 * POS, WIDTH), BF16),
            jax.ShapeDtypeStruct((WIDTH // NY, WIDTH), F32),
        ),
        in_specs=[
            pl.BlockSpec(memory_space=pltpu.SMEM), hbm, hbm, hbm,
        ],
        out_specs=(vmem, vmem),
        scratch_shapes=[
            V((3, 2 * POS, WIDTH), BF16), V((2 * POS, WIDTH), BF16), V((2, POS, HALF), BF16),
            V((GW, WIDTH), BF16), V((CROSS_W, WIDTH), BF16),
            V((NY, POS, PACK), BF16), V((TV, PACK), BF16),
            V((2, POS, WIDTH), BF16), V((TV, WIDTH), BF16),
            V((3, 2, POS, CROSS_W), F32),
            V((NY, POS, 128), BF16), V((TV, 128), BF16),
            V((3, 2, POS, CROSS_W), BF16),
            V((HEADS, TV, HD), BF16), V((HEADS, TV, HD), BF16),
            V((HEADS, TV, HD), BF16), V((HEADS, TV, HD), BF16),
            V((HEADS, TV, TV), F32), V((HEADS, TV, TV), BF16), V((TV, TV), BF16),
            V((TV, 128), BF16), V((TV, 256), BF16), V((TV, 256), BF16),
            V((NY, POS, 128), BF16), V((NY, POS, 256), BF16), V((NY, POS, 256), BF16),
            V((GW, TV), BF16),
            V((320, HALF), BF16), V((320, HALF), BF16), V((BLOCKS, NX, 8, HALF), F32),
            V((NX, BLOCKS * 8, HALF), BF16), V((NX, BLOCKS * 8, HALF), BF16),
            V((NZ, 8, HALF), F32), V((NZ, 8, HALF), BF16), V((NZ, 8, HALF), BF16),
            V((8, HALF), BF16), V((2, 8, HALF), BF16), V((2, NX, OWNED, 8, HALF), BF16),
            S((6,)), S((NY,)), S((NY,)),
            S((2, 6)), S((2, 6)), S((2, 2)), S((2, NY)), S((2,)),
            S((NY,)), S((NY,)),
            S((NY,)), S((NY,)), S((NY,)), S((NY,)), S((NY,)), S((NY,)), S((8,)), S, S, S((NX,)), S((NX,)),
            S((NZ,)), S((NZ,)), S, S((2,)), S((NZ,)), S((OWNED,)), S((NX,)), S((NX,)), S((NX,)), S((NX,)),
        ],
        compiler_params=pltpu.CompilerParams(
            collective_id=0, has_side_effects=True, vmem_limit_bytes=30 * 1024 * 1024
        ),
        name="layer",
    )(view_counts, *(pltpu.with_memory_space_constraint(a, pltpu.HBM) for a in (qkv, out_cotangent, out_weight)))


def solution(mesh):
    in_specs = (P(None, ("scene", "seq"), None), P("scene"), P(), P(("scene", "seq"), None))
    out_specs = (P(None, ("scene", "seq"), None), P("seq", None))
    return jax.shard_map(
        on_device, mesh=mesh, in_specs=in_specs, out_specs=out_specs, check_vma=False
    )
```

```python
import functools
import math

import jax
import jax.numpy as jnp
from jax import lax
from jax.experimental import pallas as pl
from jax.experimental.pallas import tpu as pltpu
from jax.sharding import PartitionSpec as P

MESH = pl.DeviceIdType.MESH
F32 = jnp.float32
BF16 = jnp.bfloat16
NT = (((1,), (1,)), ((), ()))
TN = (((0,), (0,)), ((), ()))
NN = (((1,), (0,)), ((), ()))

HD = 64
NY, NX, NZ = 8, 4, 12
GROUPS = 4
HEADS = 3
POS = 64
TV = POS * NY
VIEW_W = 768
CROSS_W = 512
WIDTH = 1280
GW = HEADS * HD
HALF = WIDTH // 2
BLOCKS = 10
OWNED = 5


def dot(a, b, dims=NN):
    return lax.dot_general(a, b, dims, preferred_element_type=F32)


def kernel(
    vc_ref, qkv_hbm, cot_hbm, w_ref, d_ref, wg_ref,
    qkv_ref, cot_ref, rel,
    wv, wc, qs, qr, qe, qx, cs, cr, cx, xs, xr, cg, hq, hk, hv, hg, pf, pr, dt, da, db, dc, ra, rb, rc, ot,
    ws, wr, wown, x_s, x_r, zown, zs, zr, yb, yr, fc,
    wsem, q_ss, q_rs, e_ss, e_rs, c_lo, c_hi, c_out, c_rs, rel_rs, x_ss, x_rs, da_ss, da_rs, db_ss, db_rs, dc_ss, dc_rs, own_s, k_ss, k_rs, xx_ss, xx_rs,
    z_ss, z_rs, y_ss, y_rs, za_ss, za_rs, xa_ss, xa_rs, ka_ss, ka_rs,
):
    scene = lax.axis_index("scene")
    y = lax.axis_index("seq")
    c = lax.rem(scene, 2)
    x = lax.rem(lax.div(scene, 2), NX)
    z = lax.div(scene, 2 * NX)
    view = lax.div(y, GROUPS)
    group = lax.rem(y, GROUPS)

    def y_at(d):
        return lax.rem(y + d, NY)

    def z_at(d):
        return lax.rem(z + d, NZ)

    def x_at(d):
        return lax.rem(x + d, NX)

    def to_y(p):
        return {"seq": p}

    def to_scene(zz, xx, cc):
        return {"scene": (zz * NX + xx) * 2 + cc}

    core_peer = to_scene(z, x, 1 - c)

    def remote(src, dst, ssem, rsem, dev):
        return pltpu.make_async_remote_copy(
            src_ref=src, dst_ref=dst, send_sem=ssem, recv_sem=rsem, device_id=dev,
            device_id_type=MESH,
        )

    barrier = pltpu.get_barrier_semaphore()
    peers = [to_y(y_at(d)) for d in range(1, NY)]
    peers += [core_peer]
    peers += [to_scene(z, x_at(d), c) for d in range(1, NX)]
    peers += [to_scene(z_at(d), x, c) for d in range(1, NZ)]
    for peer in peers:
        pl.semaphore_signal(barrier, inc=1, device_id=peer, device_id_type=MESH)
    w_view = pltpu.make_async_copy(
        w_ref.at[pl.ds(pl.multiple_of(group * GW, GW), GW)], wv, wsem.at[0]
    )
    w_cross = pltpu.make_async_copy(w_ref.at[pl.ds(VIEW_W, CROSS_W)], wc, wsem.at[1])
    for k in range(3):
        pltpu.make_async_copy(qkv_hbm.at[k], qkv_ref.at[k], wsem.at[2 + k]).start()
    cot_in = pltpu.make_async_copy(cot_hbm, cot_ref, wsem.at[5])
    cot_in.start()
    w_cross.start()
    w_view.start()

    vc = vc_ref[0]
    live = [jnp.where(vc > v, 1.0, 0.0).astype(F32) for v in range(2)]
    my_live = jnp.where(vc > view, 1.0, 0.0).astype(F32)

    def rows_of(ref, p):
        return ref.at[pl.ds(pl.multiple_of(p * POS, POS), POS)]

    def extra_of(ref, p):
        return ref.at[pl.ds(pl.multiple_of(p * (POS // 2), POS // 2), POS // 2)]

    def q_send(p):
        return (
            remote(qs.at[p], rows_of(qr, y), q_ss.at[p], q_rs.at[y], to_y(p)),
            remote(qe.at[p], extra_of(qx, y), e_ss.at[p], e_rs.at[y], to_y(p)),
        )

    def q_arrives(p):
        main, extra = rows_of(qr, p), extra_of(qx, p)
        remote(main, main, q_ss.at[0], q_rs.at[p], to_y(p)).wait_recv()
        remote(extra, extra, e_ss.at[0], e_rs.at[p], to_y(p)).wait_recv()

    row = lax.broadcasted_iota(jnp.int32, (POS, 2 * POS), 0)
    col = lax.broadcasted_iota(jnp.int32, (POS, 2 * POS), 1)
    for k in range(3):
        pltpu.make_async_copy(qkv_hbm.at[k], qkv_ref.at[k], wsem.at[2 + k]).wait()
    for v in range(2):
        pick = jnp.where(col == 2 * row + v, 1.0, 0.0).astype(BF16)
        parts = []
        for k in range(3):
            parts.append(dot(pick, qkv_ref[k, :, :VIEW_W]))
        for g in range(GROUPS):
            cols = slice(g * GW, (g + 1) * GW)
            last = parts[2][:, cols]
            packed = jnp.concatenate(
                [parts[0][:, cols], parts[1][:, cols], last[:, : 2 * HD]], axis=1
            )
            qs[v * GROUPS + g] = packed.astype(BF16)
            tail = last[:, 2 * HD :]
            qe[v * GROUPS + g] = jnp.concatenate(
                [tail[: POS // 2], tail[POS // 2 :]], axis=1
            ).astype(BF16)
        if v == 0:
            pl.semaphore_wait(barrier, len(peers))
        for p in range(v * GROUPS, (v + 1) * GROUPS):

            @pl.when(p != y)
            def _():
                for part in q_send(p):
                    part.start()


    place_in = lax.rem(y, GROUPS)
    down, up = to_y(y_at(NY - 1)), to_y(y_at(1))

    def half_of(ref, p, h):
        return ref.at[pl.ds(pl.multiple_of(p * POS, POS), POS), pl.ds(h * HALF, HALF)]

    def sorted_rows(v, h):
        return cs.at[v, :, pl.ds(h * HALF, HALF)]

    def go_down(k, h):
        s = y_at(k)
        src = sorted_rows(view, h) if k == 0 else half_of(cr, s, h)
        return remote(src, half_of(cr, s, h), c_lo.at[h, k], c_rs.at[h, s], down)

    def go_up(k, h):
        s = y_at(NY - k)
        src = sorted_rows(view, h) if k == 0 else half_of(cr, s, h)
        return remote(src, half_of(cr, s, h), c_hi.at[h, k], c_rs.at[h, s], up)

    def arrives(s, h):
        return remote(half_of(cr, s, h), half_of(cr, s, h), c_lo.at[h, 0], c_rs.at[h, s], up)

    def enter(n, h):
        mine, relayed = sorted_rows(1 - view, h), rel.at[h]
        if n == 0:
            return remote(mine, half_of(cr, y, h), c_out.at[h, 0], c_rs.at[h, y], down)
        if n == 1:
            return remote(mine, relayed, c_out.at[h, 0], rel_rs.at[h], down)
        if n == 2:
            return remote(mine, relayed, c_out.at[h, 0], rel_rs.at[h], up)
        return remote(mine, half_of(cr, y, h), c_out.at[h, 0], c_rs.at[h, y], up)

    def relay(n, h):
        s, to = (y_at(1), down) if n == 0 else (y_at(NY - 1), up)
        return remote(rel.at[h], half_of(cr, s, h), c_out.at[h, 1], c_rs.at[h, s], to)

    def relay_in(h):
        return remote(rel.at[h], rel.at[h], c_out.at[h, 1], rel_rs.at[h], up)

    def cot_start(h):
        @pl.when(place_in >= 1)
        def _():
            go_down(0, h).start()

        @pl.when(place_in <= 2)
        def _():
            go_up(0, h).start()

        for n in range(GROUPS):

            @pl.when(place_in == n)
            def _():
                enter(n, h).start()

    def cot_relay():
        for n in (0, 3):

            @pl.when(place_in == n)
            def _():
                for h in range(2):
                    relay_in(h).wait_recv()
                    relay(n, h).start()

    def cot_flow(hops):
        for k in hops:
            for h in range(2):

                @pl.when(place_in <= 5 - k)
                def _():
                    arrives(y_at(k), h).wait_recv()

                    @pl.when(place_in >= 1)
                    def _():
                        go_down(k, h).start()

                @pl.when(place_in >= k - 2)
                def _():
                    arrives(y_at(NY - k), h).wait_recv()

                    @pl.when(place_in <= 2)
                    def _():
                        go_up(k, h).start()

    def cot_end(h):
        for n in range(GROUPS):

            @pl.when(place_in == n)
            def _():
                enter(n, h).wait_send()

        for n in (0, 3):

            @pl.when(place_in == n)
            def _():
                relay(n, h).wait_send()

        for k in range(6):

            @pl.when(jnp.logical_and(place_in <= 5 - k, place_in >= 1))
            def _():
                go_down(k, h).wait_send()

            @pl.when(jnp.logical_and(place_in >= k - 2, place_in <= 2))
            def _():
                go_up(k, h).wait_send()

    def x_copy(d, mine):
        p = y_at(d)
        at = y if mine else p
        return remote(xs.at[p], rows_of(xr, at), x_ss.at[d], x_rs.at[at], to_y(p))

    returned = [(da, ra, da_ss, da_rs), (db, rb, db_ss, db_rs), (dc, rc, dc_ss, dc_rs)]

    def d_copy(n, d, mine):
        src, dst, ssem, rsem = returned[n]
        p = y_at(d)
        at = y if mine else p
        return remote(rows_of(src, p), dst.at[at], ssem.at[d], rsem.at[at], to_y(p))

    d_own = [
        pltpu.make_async_copy(rows_of(src, y), dst.at[y], own_s.at[5 + n])
        for n, (src, dst, _, _) in enumerate(returned)
    ]

    q_own = pltpu.make_async_copy(qs.at[y], rows_of(qr, y), own_s.at[0])
    e_own = pltpu.make_async_copy(qe.at[y], extra_of(qx, y), own_s.at[3])
    c_own = pltpu.make_async_copy(cs.at[view], rows_of(cr, y), own_s.at[1])
    x_own = pltpu.make_async_copy(xs.at[y], rows_of(xr, y), own_s.at[2])

    q_own.start()
    e_own.start()
    cot_in.wait()
    for v in range(2):
        pick = jnp.where(col == 2 * row + v, 1.0, 0.0).astype(BF16)
        cs[v] = dot(pick, cot_ref[...]).astype(BF16)
    for h in range(2):
        cot_start(h)
    c_own.start()
    for v in range(2):
        pick = jnp.where(col == 2 * row + v, 1.0, 0.0).astype(BF16)
        for k in range(3):
            cx[k, v] = dot(pick, qkv_ref[k, :, VIEW_W:])

    w_cross.wait()
    same = jnp.where(
        lax.broadcasted_iota(jnp.int32, (CROSS_W, CROSS_W), 0) // HD
        == lax.broadcasted_iota(jnp.int32, (CROSS_W, CROSS_W), 1) // HD,
        1.0,
        0.0,
    ).astype(BF16)

    def head_sum(t):
        hi = t.astype(BF16)
        lo = (t - hi.astype(F32)).astype(BF16)
        return dot(hi, same) + dot(lo, same)

    scale = 1.0 / math.sqrt(HD)
    gs = []
    for v in range(2):
        g = dot(cs[v], wc[...], NT).astype(BF16).astype(F32)
        gs.append(g * live[v])
    dq = []
    dk = [None, None]
    dv = [None, None]
    for a in range(2):
        q = cx[0, a]
        s0 = head_sum(q * cx[1, 0]) * scale
        s1 = head_sum(q * cx[1, 1]) * scale
        s1 = jnp.where(live[1] > 0.5, s1, -1e30)
        m = jnp.maximum(s0, s1)
        e0 = jnp.exp(s0 - m)
        e1 = jnp.exp(s1 - m)
        inv = 1.0 / (e0 + e1)
        p = [e0 * inv, e1 * inv]
        pb = [t.astype(BF16).astype(F32) for t in p]
        out = ((pb[0] * cx[2, 0] + pb[1] * cx[2, 1]) * live[a]).astype(BF16)
        for g in range(GROUPS):
            xs[a * GROUPS + g] = out[:, g * 128 : (g + 1) * 128]
        dp = [head_sum(gs[a] * cx[2, b]) for b in range(2)]
        mean = p[0] * dp[0] + p[1] * dp[1]
        grad = [p[b] * (dp[b] - mean) * scale for b in range(2)]
        dq.append(grad[0] * cx[1, 0] + grad[1] * cx[1, 1])
        for b in range(2):
            tk = grad[b] * q
            tv = pb[b] * gs[a]
            dk[b] = tk if dk[b] is None else dk[b] + tk
            dv[b] = tv if dv[b] is None else dv[b] + tv
    for d in range(1, NY):
        x_copy(d, True).start()
    x_own.start()
    for v in range(2):
        cg[0, v] = dq[v].astype(BF16)
        cg[1, v] = dk[v].astype(BF16)
        cg[2, v] = dv[v].astype(BF16)

    for d in range(1, NY):
        q_arrives(y_at(d))
    q_own.wait()
    e_own.wait()
    packed = qr[...]
    for h in range(HEADS):
        hq[h] = packed[:, h * HD : (h + 1) * HD]
        hk[h] = packed[:, GW + h * HD : GW + (h + 1) * HD]
        if h < 2:
            hv[h] = packed[:, 2 * GW + h * HD : 2 * GW + (h + 1) * HD]
    extra = qx[...].reshape(NY, POS // 2, 2 * HD)
    hv[2] = jnp.concatenate([extra[:, :, :HD], extra[:, :, HD:]], axis=1).reshape(TV, HD)
    chunk = 128

    def forward(h, carry):
        k = hk[h]
        v = hv[h]
        for i in range(TV // chunk):
            at = slice(i * chunk, (i + 1) * chunk)
            s = dot(k, hq[h, at, :], NT) * scale
            e = jnp.exp(s - jnp.max(s, axis=0, keepdims=True))
            p = e * (1.0 / jnp.sum(e, axis=0, keepdims=True))
            pf[h, :, at] = p
            pr[h, :, at] = p.astype(BF16)
        ot[pl.ds(pl.multiple_of(h * HD, HD), HD), :] = (dot(v, pr[h], TN) * my_live).astype(BF16)
        return carry

    lax.fori_loop(0, HEADS, forward, 0)

    def backward(h):
        k = hk[h]
        v = hv[h]
        for i in range(TV // chunk):
            at = slice(i * chunk, (i + 1) * chunk)
            p = pf[h, :, at]
            dp = dot(v, hg[h, at, :], NT)
            mean = jnp.sum(p * dp, axis=0, keepdims=True)
            dt[:, at] = (p * (dp - mean) * scale).astype(BF16)
        grads = dt[...]
        return dot(k, grads, TN).T, dot(grads, hq[h]), dot(pr[h], hg[h])

    cot_relay()
    cot_flow((1, 2, 3))
    for d in range(1, NY):
        x_copy(d, False).wait_recv()
    x_own.wait()
    ot[GW:, :] = xr[...].astype(F32).T.astype(BF16)
    cot_flow((4, 5))
    c_own.wait()

    def partial(cc):
        cols = pl.ds(pl.multiple_of(cc * HALF, HALF), HALF)
        return dot(ot[...], cr[:, cols])

    ws[...] = partial(1 - c).astype(BF16)
    k_copy = remote(ws, wr, k_ss, k_rs, core_peer)
    k_copy.start()
    wown[...] = partial(c).reshape(BLOCKS, NX, 8, HALF)

    k_copy.wait_recv()
    wown[...] = wown[...] + wr[...].astype(F32).reshape(BLOCKS, NX, 8, HALF)
    for i in range(NX):
        x_s[i] = wown[:, i].reshape(BLOCKS * 8, HALF).astype(BF16)

    def xx_copy(d, mine):
        p = x_at(d)
        at = x if mine else p
        return remote(x_s.at[p], x_r.at[at], xx_ss.at[d], xx_rs.at[at], to_scene(z, p, c))

    for d in range(1, NX):
        xx_copy(d, True).start()
    w_view.wait()
    g_all = (dot(cr[...], wv[...], NT).astype(BF16).astype(F32) * my_live).astype(BF16)
    for h in range(HEADS):
        hg[h] = g_all[:, h * HD : (h + 1) * HD]
    dq0, dk0, dv0 = backward(0)
    da[...] = jnp.concatenate([dq0, dk0], axis=1).astype(BF16)
    db[:, 2 * HD : 3 * HD] = dv0.astype(BF16)
    for d in range(1, NY):
        d_copy(0, d, True).start()
    d_own[0].start()

    dq1, dk1, dv1 = backward(1)
    db[:, : 2 * HD] = jnp.concatenate([dq1, dk1], axis=1).astype(BF16)
    db[:, 3 * HD :] = dv1.astype(BF16)
    for d in range(1, NY):
        d_copy(1, d, True).start()
    d_own[1].start()
    total = wown[:, x].reshape(BLOCKS * 8, HALF)
    for d in range(1, NX):
        xx_copy(d, False).wait_recv()
        total = total + x_r[x_at(d)].astype(F32)
    zown[:BLOCKS] = total.reshape(BLOCKS, 8, HALF)
    for j in range(BLOCKS):
        zs[j] = total[8 * j : 8 * j + 8].astype(BF16)

    def local_block(zz):
        late = lax.div(zz, 6)
        return (1 - late) * zz + late * (6 + lax.rem(zz + 24 - 4 * group, 6))

    def z_copy(d, mine):
        p = z_at(d)
        at = z if mine else p
        return remote(zs.at[local_block(p)], zr.at[at], z_ss.at[d], z_rs.at[at], to_scene(p, x, c))

    for d in range(1, NZ):

        @pl.when(local_block(z_at(d)) < BLOCKS)
        def _():
            z_copy(d, True).start()

    dq2, dk2, dv2 = backward(2)
    dc[...] = jnp.concatenate([dq2, dk2, dv2, jnp.zeros((TV, HD), F32)], axis=1).astype(BF16)
    late = lax.div(z, 6)
    mine_at = local_block(z)
    blk = (1 - late) * (6 * group + mine_at) + late * (18 + 4 * group + mine_at)
    owner = lax.div(blk, OWNED)
    y_copy = remote(yb, yr.at[view], y_ss, y_rs.at[view], to_y(owner))
    y_own = pltpu.make_async_copy(yb, yr.at[view], own_s.at[4])
    away = jnp.logical_and(mine_at < BLOCKS, owner != y)
    here = jnp.logical_and(mine_at < BLOCKS, owner == y)

    @pl.when(mine_at < BLOCKS)
    def _():
        acc = zown[mine_at]
        for d in range(1, NZ):
            z_copy(d, False).wait_recv()
            acc = acc + zr[z_at(d)].astype(F32)
        yb[...] = acc.astype(BF16)

    @pl.when(away)
    def _():
        y_copy.start()

    @pl.when(here)
    def _():
        y_own.start()

    for d in range(1, NY):
        d_copy(2, d, True).start()
    d_own[2].start()

    tokens = TV * 2 * NZ * NX * 2
    slots = []
    for i in range(OWNED):
        b = y * OWNED + i
        high = lax.div(b, 24)
        rest = b - 24 * high
        src_group = (1 - high) * lax.div(rest, 6) + high * lax.div(rest, 4)
        src_z = 6 * high + lax.rem(b, 6)
        slots.append((src_group, src_z))

    def za_copy(i, d):
        piece = fc.at[c, x, i]
        return remote(piece, piece, za_ss.at[d], za_rs.at[i], to_scene(z_at(d), x, c))

    for i, (src_group, src_z) in enumerate(slots):

        @pl.when(src_z == z)
        def _():
            for v in range(2):
                src_y = v * GROUPS + src_group

                @pl.when(src_y != y)
                def _():
                    remote(yb, yr.at[v], y_ss, y_rs.at[v], to_y(src_y)).wait_recv()

                @pl.when(src_y == y)
                def _():
                    pltpu.make_async_copy(yb, yr.at[v], own_s.at[4]).wait()

            both = yr[0].astype(F32) + yr[1].astype(F32)
            fc[c, x, i] = (both * (1.0 / math.sqrt(tokens))).astype(BF16)
            for d in range(1, NZ):
                za_copy(i, d).start()

    for n in range(3):
        for d in range(1, NY):
            d_copy(n, d, False).wait_recv()
        d_own[n].wait()
    trow = lax.broadcasted_iota(jnp.int32, (2 * POS, POS), 0)
    tcol = lax.broadcasted_iota(jnp.int32, (2 * POS, POS), 1)
    place = [jnp.where(trow == 2 * tcol + v, 1.0, 0.0).astype(BF16) for v in range(2)]
    homes = [
        [(ra, 0), (rb, 0), (rc, 0)],
        [(ra, HD), (rb, HD), (rc, HD)],
        [(rb, 2 * HD), (rb, 3 * HD), (rc, 2 * HD)],
    ]
    for k in range(3):
        acc = None
        for v in range(2):
            view_part = jnp.concatenate(
                [
                    ref[v * GROUPS + g][:, lane : lane + HD].astype(F32)
                    for g in range(GROUPS)
                    for ref, lane in homes[k]
                ],
                axis=1,
            ).astype(BF16)
            full = jnp.concatenate([view_part, cg[k, v]], axis=1)
            t = dot(place[v], full)
            acc = t if acc is None else acc + t
        d_ref[k] = acc.astype(BF16)

    for i, (_, src_z) in enumerate(slots):

        @pl.when(src_z != z)
        def _():
            za_copy(i, 1).wait_recv()

    def xa_copy(d, mine):
        p = x_at(d)
        piece = fc.at[c, x if mine else p]
        return remote(piece, piece, xa_ss.at[d], xa_rs.at[x if mine else p], to_scene(z, p, c))

    def ka_copy(cc, xx):
        return remote(fc.at[cc, xx], fc.at[cc, xx], ka_ss.at[xx], ka_rs.at[xx], core_peer)

    for d in range(1, NX):
        xa_copy(d, True).start()
    ka_copy(c, x).start()
    for d in (1, 3, 2):
        xa_copy(d, False).wait_recv()
        ka_copy(c, x_at(d)).start()
    for xx in range(NX):
        ka_copy(1 - c, xx).wait_recv()
    for cc in range(2):
        for xx in range(NX):
            for i in range(OWNED):
                at = 32 * i + 8 * xx
                wg_ref[at : at + 8, cc * HALF : (cc + 1) * HALF] = fc[cc, xx, i].astype(F32)

    for p in range(NY):

        @pl.when(p != y)
        def _():
            for part in q_send(p):
                part.wait_send()

    for h in range(2):
        cot_end(h)
    for d in range(1, NY):
        x_copy(d, True).wait_send()
        for n in range(3):
            d_copy(n, d, True).wait_send()
    k_copy.wait_send()
    for d in range(1, NX):
        xx_copy(d, True).wait_send()
        xa_copy(d, True).wait_send()
    for d in range(1, NZ):

        @pl.when(local_block(z_at(d)) < BLOCKS)
        def _():
            z_copy(d, True).wait_send()

    @pl.when(away)
    def _():
        y_copy.wait_send()

    for i, (_, src_z) in enumerate(slots):

        @pl.when(src_z == z)
        def _():
            for d in range(1, NZ):
                za_copy(i, d).wait_send()

    for xx in range(NX):
        ka_copy(c, xx).wait_send()


def on_device(qkv, view_counts, out_weight, out_cotangent):
    vmem = pl.BlockSpec(memory_space=pltpu.VMEM)
    hbm = pl.BlockSpec(memory_space=pltpu.HBM)
    V = pltpu.VMEM
    S = pltpu.SemaphoreType.DMA
    return pl.pallas_call(
        kernel,
        out_shape=(
            jax.ShapeDtypeStruct((3, 2 * POS, WIDTH), BF16),
            jax.ShapeDtypeStruct((WIDTH // NY, WIDTH), F32),
        ),
        in_specs=[
            pl.BlockSpec(memory_space=pltpu.SMEM), hbm, hbm, hbm,
        ],
        out_specs=(vmem, vmem),
        scratch_shapes=[
            V((3, 2 * POS, WIDTH), BF16), V((2 * POS, WIDTH), BF16), V((2, POS, HALF), BF16),
            V((GW, WIDTH), BF16), V((CROSS_W, WIDTH), BF16),
            V((NY, POS, 512), BF16), V((TV, 512), BF16),
            V((NY, POS // 2, 128), BF16), V((TV // 2, 128), BF16),
            V((2, POS, WIDTH), BF16), V((TV, WIDTH), BF16),
            V((3, 2, POS, CROSS_W), F32),
            V((NY, POS, 128), BF16), V((TV, 128), BF16),
            V((3, 2, POS, CROSS_W), BF16),
            V((HEADS, TV, HD), BF16), V((HEADS, TV, HD), BF16),
            V((HEADS, TV, HD), BF16), V((HEADS, TV, HD), BF16),
            V((HEADS, TV, TV), F32), V((HEADS, TV, TV), BF16), V((TV, TV), BF16),
            V((TV, 128), BF16), V((TV, 256), BF16), V((TV, 256), BF16),
            V((NY, POS, 128), BF16), V((NY, POS, 256), BF16), V((NY, POS, 256), BF16),
            V((320, TV), BF16),
            V((320, HALF), BF16), V((320, HALF), BF16), V((BLOCKS, NX, 8, HALF), F32),
            V((NX, BLOCKS * 8, HALF), BF16), V((NX, BLOCKS * 8, HALF), BF16),
            V((NZ, 8, HALF), F32), V((NZ, 8, HALF), BF16), V((NZ, 8, HALF), BF16),
            V((8, HALF), BF16), V((2, 8, HALF), BF16), V((2, NX, OWNED, 8, HALF), BF16),
            S((6,)), S((NY,)), S((NY,)), S((NY,)), S((NY,)),
            S((2, 6)), S((2, 6)), S((2, 2)), S((2, NY)), S((2,)),
            S((NY,)), S((NY,)),
            S((NY,)), S((NY,)), S((NY,)), S((NY,)), S((NY,)), S((NY,)), S((8,)), S, S, S((NX,)), S((NX,)),
            S((NZ,)), S((NZ,)), S, S((2,)), S((NZ,)), S((OWNED,)), S((NX,)), S((NX,)), S((NX,)), S((NX,)),
        ],
        compiler_params=pltpu.CompilerParams(
            collective_id=0, has_side_effects=True, vmem_limit_bytes=30 * 1024 * 1024
        ),
        name="layer",
    )(view_counts, *(pltpu.with_memory_space_constraint(a, pltpu.HBM) for a in (qkv, out_cotangent, out_weight)))


def solution(mesh):
    in_specs = (P(None, ("scene", "seq"), None), P("scene"), P(), P(("scene", "seq"), None))
    out_specs = (P(None, ("scene", "seq"), None), P("seq", None))
    return jax.shard_map(
        on_device, mesh=mesh, in_specs=in_specs, out_specs=out_specs, check_vma=False
    )
```

```python
import functools
import math

import jax
import jax.numpy as jnp
from jax import lax
from jax.experimental import pallas as pl
from jax.experimental.pallas import tpu as pltpu
from jax.sharding import PartitionSpec as P

MESH = pl.DeviceIdType.MESH
F32 = jnp.float32
BF16 = jnp.bfloat16
NT = (((1,), (1,)), ((), ()))
TN = (((0,), (0,)), ((), ()))
NN = (((1,), (0,)), ((), ()))

HD = 64
NY, NX, NZ = 8, 4, 12
GROUPS = 4
HEADS = 3
POS = 64
TV = POS * NY
VIEW_W = 768
CROSS_W = 512
WIDTH = 1280
GW = HEADS * HD
HALF = WIDTH // 2
BLOCKS = 10
OWNED = 5


def dot(a, b, dims=NN):
    return lax.dot_general(a, b, dims, preferred_element_type=F32)


def kernel(
    vc_ref, qkv_hbm, cot_hbm, w_ref, d_ref, wg_ref,
    qkv_ref, cot_ref, rel,
    wv, wc, qs, qr, qe, qx, cs, cr, cx, xs, xr, cg, hq, hk, hv, hg, pf, pr, dt, da, db, dc, ra, rb, rc, ot,
    ws, wr, wown, x_s, x_r, zown, zs, zr, yb, yr, fc,
    wsem, q_ss, q_rs, e_ss, e_rs, c_lo, c_hi, c_out, c_rs, rel_rs, x_ss, x_rs, da_ss, da_rs, db_ss, db_rs, dc_ss, dc_rs, own_s, k_ss, k_rs, xx_ss, xx_rs,
    z_ss, z_rs, y_ss, y_rs, za_ss, za_rs, xa_ss, xa_rs, ka_ss, ka_rs,
):
    scene = lax.axis_index("scene")
    y = lax.axis_index("seq")
    c = lax.rem(scene, 2)
    x = lax.rem(lax.div(scene, 2), NX)
    z = lax.div(scene, 2 * NX)
    view = lax.div(y, GROUPS)
    group = lax.rem(y, GROUPS)

    def y_at(d):
        return lax.rem(y + d, NY)

    def z_at(d):
        return lax.rem(z + d, NZ)

    def x_at(d):
        return lax.rem(x + d, NX)

    def to_y(p):
        return {"seq": p}

    def to_scene(zz, xx, cc):
        return {"scene": (zz * NX + xx) * 2 + cc}

    core_peer = to_scene(z, x, 1 - c)

    def remote(src, dst, ssem, rsem, dev):
        return pltpu.make_async_remote_copy(
            src_ref=src, dst_ref=dst, send_sem=ssem, recv_sem=rsem, device_id=dev,
            device_id_type=MESH,
        )

    barrier = pltpu.get_barrier_semaphore()
    peers = [to_y(y_at(d)) for d in range(1, NY)]
    peers += [core_peer]
    peers += [to_scene(z, x_at(d), c) for d in range(1, NX)]
    peers += [to_scene(z_at(d), x, c) for d in range(1, NZ)]
    for peer in peers:
        pl.semaphore_signal(barrier, inc=1, device_id=peer, device_id_type=MESH)
    w_view = pltpu.make_async_copy(
        w_ref.at[pl.ds(pl.multiple_of(group * GW, GW), GW)], wv, wsem.at[0]
    )
    w_cross = pltpu.make_async_copy(w_ref.at[pl.ds(VIEW_W, CROSS_W)], wc, wsem.at[1])
    cot_in = pltpu.make_async_copy(cot_hbm, cot_ref, wsem.at[5])
    cot_in.start()
    for k in range(3):
        pltpu.make_async_copy(qkv_hbm.at[k], qkv_ref.at[k], wsem.at[2 + k]).start()
    w_cross.start()
    w_view.start()

    vc = vc_ref[0]
    live = [jnp.where(vc > v, 1.0, 0.0).astype(F32) for v in range(2)]
    my_live = jnp.where(vc > view, 1.0, 0.0).astype(F32)

    def rows_of(ref, p):
        return ref.at[pl.ds(pl.multiple_of(p * POS, POS), POS)]

    def extra_of(ref, p):
        return ref.at[pl.ds(pl.multiple_of(p * (POS // 2), POS // 2), POS // 2)]

    def q_send(p):
        return (
            remote(qs.at[p], rows_of(qr, y), q_ss.at[p], q_rs.at[y], to_y(p)),
            remote(qe.at[p], extra_of(qx, y), e_ss.at[p], e_rs.at[y], to_y(p)),
        )

    def q_arrives(p):
        main, extra = rows_of(qr, p), extra_of(qx, p)
        remote(main, main, q_ss.at[0], q_rs.at[p], to_y(p)).wait_recv()
        remote(extra, extra, e_ss.at[0], e_rs.at[p], to_y(p)).wait_recv()

    row = lax.broadcasted_iota(jnp.int32, (POS, 2 * POS), 0)
    col = lax.broadcasted_iota(jnp.int32, (POS, 2 * POS), 1)
    place_in = lax.rem(y, GROUPS)
    down, up = to_y(y_at(NY - 1)), to_y(y_at(1))

    def half_of(ref, p, h):
        return ref.at[pl.ds(pl.multiple_of(p * POS, POS), POS), pl.ds(h * HALF, HALF)]

    def sorted_rows(v, h):
        return cs.at[v, :, pl.ds(h * HALF, HALF)]

    def go_down(k, h):
        s = y_at(k)
        src = sorted_rows(view, h) if k == 0 else half_of(cr, s, h)
        return remote(src, half_of(cr, s, h), c_lo.at[h, k], c_rs.at[h, s], down)

    def go_up(k, h):
        s = y_at(NY - k)
        src = sorted_rows(view, h) if k == 0 else half_of(cr, s, h)
        return remote(src, half_of(cr, s, h), c_hi.at[h, k], c_rs.at[h, s], up)

    def arrives(s, h):
        return remote(half_of(cr, s, h), half_of(cr, s, h), c_lo.at[h, 0], c_rs.at[h, s], up)

    def enter(n, h):
        mine, relayed = sorted_rows(1 - view, h), rel.at[h]
        if n == 0:
            return remote(mine, half_of(cr, y, h), c_out.at[h, 0], c_rs.at[h, y], down)
        if n == 1:
            return remote(mine, relayed, c_out.at[h, 0], rel_rs.at[h], down)
        if n == 2:
            return remote(mine, relayed, c_out.at[h, 0], rel_rs.at[h], up)
        return remote(mine, half_of(cr, y, h), c_out.at[h, 0], c_rs.at[h, y], up)

    def relay(n, h):
        s, to = (y_at(1), down) if n == 0 else (y_at(NY - 1), up)
        return remote(rel.at[h], half_of(cr, s, h), c_out.at[h, 1], c_rs.at[h, s], to)

    def relay_in(h):
        return remote(rel.at[h], rel.at[h], c_out.at[h, 1], rel_rs.at[h], up)

    def cot_start(h):
        @pl.when(place_in >= 1)
        def _():
            go_down(0, h).start()

        @pl.when(place_in <= 2)
        def _():
            go_up(0, h).start()

        for n in range(GROUPS):

            @pl.when(place_in == n)
            def _():
                enter(n, h).start()

    def cot_relay():
        for n in (0, 3):

            @pl.when(place_in == n)
            def _():
                for h in range(2):
                    relay_in(h).wait_recv()
                    relay(n, h).start()

    def cot_flow(hops):
        for k in hops:
            for h in range(2):

                @pl.when(place_in <= 5 - k)
                def _():
                    arrives(y_at(k), h).wait_recv()

                    @pl.when(place_in >= 1)
                    def _():
                        go_down(k, h).start()

                @pl.when(place_in >= k - 2)
                def _():
                    arrives(y_at(NY - k), h).wait_recv()

                    @pl.when(place_in <= 2)
                    def _():
                        go_up(k, h).start()

    def cot_end(h):
        for n in range(GROUPS):

            @pl.when(place_in == n)
            def _():
                enter(n, h).wait_send()

        for n in (0, 3):

            @pl.when(place_in == n)
            def _():
                relay(n, h).wait_send()

        for k in range(6):

            @pl.when(jnp.logical_and(place_in <= 5 - k, place_in >= 1))
            def _():
                go_down(k, h).wait_send()

            @pl.when(jnp.logical_and(place_in >= k - 2, place_in <= 2))
            def _():
                go_up(k, h).wait_send()

    c_own = pltpu.make_async_copy(cs.at[view], rows_of(cr, y), own_s.at[1])
    cot_in.wait()
    for v in range(2):
        pick = jnp.where(col == 2 * row + v, 1.0, 0.0).astype(BF16)
        cs[v] = dot(pick, cot_ref[...]).astype(BF16)
    pl.semaphore_wait(barrier, len(peers))
    for h in range(2):
        cot_start(h)
    c_own.start()
    for k in range(3):
        pltpu.make_async_copy(qkv_hbm.at[k], qkv_ref.at[k], wsem.at[2 + k]).wait()
    for v in range(2):
        pick = jnp.where(col == 2 * row + v, 1.0, 0.0).astype(BF16)
        parts = []
        for k in range(3):
            parts.append(dot(pick, qkv_ref[k, :, :VIEW_W]))
        for g in range(GROUPS):
            cols = slice(g * GW, (g + 1) * GW)
            last = parts[2][:, cols]
            packed = jnp.concatenate(
                [parts[0][:, cols], parts[1][:, cols], last[:, : 2 * HD]], axis=1
            )
            qs[v * GROUPS + g] = packed.astype(BF16)
            tail = last[:, 2 * HD :]
            qe[v * GROUPS + g] = jnp.concatenate(
                [tail[: POS // 2], tail[POS // 2 :]], axis=1
            ).astype(BF16)
        for p in range(v * GROUPS, (v + 1) * GROUPS):

            @pl.when(p != y)
            def _():
                for part in q_send(p):
                    part.start()


    def x_copy(d, mine):
        p = y_at(d)
        at = y if mine else p
        return remote(xs.at[p], rows_of(xr, at), x_ss.at[d], x_rs.at[at], to_y(p))

    returned = [(da, ra, da_ss, da_rs), (db, rb, db_ss, db_rs), (dc, rc, dc_ss, dc_rs)]

    def d_copy(n, d, mine):
        src, dst, ssem, rsem = returned[n]
        p = y_at(d)
        at = y if mine else p
        return remote(rows_of(src, p), dst.at[at], ssem.at[d], rsem.at[at], to_y(p))

    d_own = [
        pltpu.make_async_copy(rows_of(src, y), dst.at[y], own_s.at[5 + n])
        for n, (src, dst, _, _) in enumerate(returned)
    ]

    q_own = pltpu.make_async_copy(qs.at[y], rows_of(qr, y), own_s.at[0])
    e_own = pltpu.make_async_copy(qe.at[y], extra_of(qx, y), own_s.at[3])
    x_own = pltpu.make_async_copy(xs.at[y], rows_of(xr, y), own_s.at[2])

    q_own.start()
    e_own.start()
    for v in range(2):
        pick = jnp.where(col == 2 * row + v, 1.0, 0.0).astype(BF16)
        for k in range(3):
            cx[k, v] = dot(pick, qkv_ref[k, :, VIEW_W:])

    w_cross.wait()
    same = jnp.where(
        lax.broadcasted_iota(jnp.int32, (CROSS_W, CROSS_W), 0) // HD
        == lax.broadcasted_iota(jnp.int32, (CROSS_W, CROSS_W), 1) // HD,
        1.0,
        0.0,
    ).astype(BF16)

    def head_sum(t):
        hi = t.astype(BF16)
        lo = (t - hi.astype(F32)).astype(BF16)
        return dot(hi, same) + dot(lo, same)

    scale = 1.0 / math.sqrt(HD)
    gs = []
    for v in range(2):
        g = dot(cs[v], wc[...], NT).astype(BF16).astype(F32)
        gs.append(g * live[v])
    dq = []
    dk = [None, None]
    dv = [None, None]
    for a in range(2):
        q = cx[0, a]
        s0 = head_sum(q * cx[1, 0]) * scale
        s1 = head_sum(q * cx[1, 1]) * scale
        s1 = jnp.where(live[1] > 0.5, s1, -1e30)
        m = jnp.maximum(s0, s1)
        e0 = jnp.exp(s0 - m)
        e1 = jnp.exp(s1 - m)
        inv = 1.0 / (e0 + e1)
        p = [e0 * inv, e1 * inv]
        pb = [t.astype(BF16).astype(F32) for t in p]
        out = ((pb[0] * cx[2, 0] + pb[1] * cx[2, 1]) * live[a]).astype(BF16)
        for g in range(GROUPS):
            xs[a * GROUPS + g] = out[:, g * 128 : (g + 1) * 128]
        dp = [head_sum(gs[a] * cx[2, b]) for b in range(2)]
        mean = p[0] * dp[0] + p[1] * dp[1]
        grad = [p[b] * (dp[b] - mean) * scale for b in range(2)]
        dq.append(grad[0] * cx[1, 0] + grad[1] * cx[1, 1])
        for b in range(2):
            tk = grad[b] * q
            tv = pb[b] * gs[a]
            dk[b] = tk if dk[b] is None else dk[b] + tk
            dv[b] = tv if dv[b] is None else dv[b] + tv
    for d in range(1, NY):
        x_copy(d, True).start()
    x_own.start()
    for v in range(2):
        cg[0, v] = dq[v].astype(BF16)
        cg[1, v] = dk[v].astype(BF16)
        cg[2, v] = dv[v].astype(BF16)

    cot_relay()
    cot_flow((1, 2))

    for d in range(1, NY):
        q_arrives(y_at(d))
    q_own.wait()
    e_own.wait()
    packed = qr[...]
    for h in range(HEADS):
        hq[h] = packed[:, h * HD : (h + 1) * HD]
        hk[h] = packed[:, GW + h * HD : GW + (h + 1) * HD]
        if h < 2:
            hv[h] = packed[:, 2 * GW + h * HD : 2 * GW + (h + 1) * HD]
    extra = qx[...].reshape(NY, POS // 2, 2 * HD)
    hv[2] = jnp.concatenate([extra[:, :, :HD], extra[:, :, HD:]], axis=1).reshape(TV, HD)
    chunk = 128

    def forward(h, carry):
        k = hk[h]
        v = hv[h]
        for i in range(TV // chunk):
            at = slice(i * chunk, (i + 1) * chunk)
            s = dot(k, hq[h, at, :], NT) * scale
            e = jnp.exp(s - jnp.max(s, axis=0, keepdims=True))
            p = e * (1.0 / jnp.sum(e, axis=0, keepdims=True))
            pf[h, :, at] = p
            pr[h, :, at] = p.astype(BF16)
        ot[pl.ds(pl.multiple_of(h * HD, HD), HD), :] = (dot(v, pr[h], TN) * my_live).astype(BF16)
        return carry

    lax.fori_loop(0, HEADS, forward, 0)

    def backward(h):
        k = hk[h]
        v = hv[h]
        for i in range(TV // chunk):
            at = slice(i * chunk, (i + 1) * chunk)
            p = pf[h, :, at]
            dp = dot(v, hg[h, at, :], NT)
            mean = jnp.sum(p * dp, axis=0, keepdims=True)
            dt[:, at] = (p * (dp - mean) * scale).astype(BF16)
        grads = dt[...]
        return dot(k, grads, TN).T, dot(grads, hq[h]), dot(pr[h], hg[h])

    cot_flow((3,))
    for d in range(1, NY):
        x_copy(d, False).wait_recv()
    x_own.wait()
    ot[GW:, :] = xr[...].astype(F32).T.astype(BF16)
    cot_flow((4, 5))
    c_own.wait()

    def partial(cc):
        cols = pl.ds(pl.multiple_of(cc * HALF, HALF), HALF)
        return dot(ot[...], cr[:, cols])

    ws[...] = partial(1 - c).astype(BF16)
    k_copy = remote(ws, wr, k_ss, k_rs, core_peer)
    k_copy.start()
    wown[...] = partial(c).reshape(BLOCKS, NX, 8, HALF)

    k_copy.wait_recv()
    wown[...] = wown[...] + wr[...].astype(F32).reshape(BLOCKS, NX, 8, HALF)
    for i in range(NX):
        x_s[i] = wown[:, i].reshape(BLOCKS * 8, HALF).astype(BF16)

    def xx_copy(d, mine):
        p = x_at(d)
        at = x if mine else p
        return remote(x_s.at[p], x_r.at[at], xx_ss.at[d], xx_rs.at[at], to_scene(z, p, c))

    for d in range(1, NX):
        xx_copy(d, True).start()
    w_view.wait()
    g_all = (dot(cr[...], wv[...], NT).astype(BF16).astype(F32) * my_live).astype(BF16)
    for h in range(HEADS):
        hg[h] = g_all[:, h * HD : (h + 1) * HD]
    dq0, dk0, dv0 = backward(0)
    da[...] = jnp.concatenate([dq0, dk0], axis=1).astype(BF16)
    db[:, 2 * HD : 3 * HD] = dv0.astype(BF16)
    for d in range(1, NY):
        d_copy(0, d, True).start()
    d_own[0].start()

    dq1, dk1, dv1 = backward(1)
    db[:, : 2 * HD] = jnp.concatenate([dq1, dk1], axis=1).astype(BF16)
    db[:, 3 * HD :] = dv1.astype(BF16)
    for d in range(1, NY):
        d_copy(1, d, True).start()
    d_own[1].start()
    total = wown[:, x].reshape(BLOCKS * 8, HALF)
    for d in range(1, NX):
        xx_copy(d, False).wait_recv()
        total = total + x_r[x_at(d)].astype(F32)
    zown[:BLOCKS] = total.reshape(BLOCKS, 8, HALF)
    for j in range(BLOCKS):
        zs[j] = total[8 * j : 8 * j + 8].astype(BF16)

    def local_block(zz):
        late = lax.div(zz, 6)
        return (1 - late) * zz + late * (6 + lax.rem(zz + 24 - 4 * group, 6))

    def z_copy(d, mine):
        p = z_at(d)
        at = z if mine else p
        return remote(zs.at[local_block(p)], zr.at[at], z_ss.at[d], z_rs.at[at], to_scene(p, x, c))

    for d in range(1, NZ):

        @pl.when(local_block(z_at(d)) < BLOCKS)
        def _():
            z_copy(d, True).start()

    dq2, dk2, dv2 = backward(2)
    dc[...] = jnp.concatenate([dq2, dk2, dv2, jnp.zeros((TV, HD), F32)], axis=1).astype(BF16)
    late = lax.div(z, 6)
    mine_at = local_block(z)
    blk = (1 - late) * (6 * group + mine_at) + late * (18 + 4 * group + mine_at)
    owner = lax.div(blk, OWNED)
    y_copy = remote(yb, yr.at[view], y_ss, y_rs.at[view], to_y(owner))
    y_own = pltpu.make_async_copy(yb, yr.at[view], own_s.at[4])
    away = jnp.logical_and(mine_at < BLOCKS, owner != y)
    here = jnp.logical_and(mine_at < BLOCKS, owner == y)

    @pl.when(mine_at < BLOCKS)
    def _():
        acc = zown[mine_at]
        for d in range(1, NZ):
            z_copy(d, False).wait_recv()
            acc = acc + zr[z_at(d)].astype(F32)
        yb[...] = acc.astype(BF16)

    @pl.when(away)
    def _():
        y_copy.start()

    @pl.when(here)
    def _():
        y_own.start()

    for d in range(1, NY):
        d_copy(2, d, True).start()
    d_own[2].start()

    tokens = TV * 2 * NZ * NX * 2
    slots = []
    for i in range(OWNED):
        b = y * OWNED + i
        high = lax.div(b, 24)
        rest = b - 24 * high
        src_group = (1 - high) * lax.div(rest, 6) + high * lax.div(rest, 4)
        src_z = 6 * high + lax.rem(b, 6)
        slots.append((src_group, src_z))

    def za_copy(i, d):
        piece = fc.at[c, x, i]
        return remote(piece, piece, za_ss.at[d], za_rs.at[i], to_scene(z_at(d), x, c))

    for i, (src_group, src_z) in enumerate(slots):

        @pl.when(src_z == z)
        def _():
            for v in range(2):
                src_y = v * GROUPS + src_group

                @pl.when(src_y != y)
                def _():
                    remote(yb, yr.at[v], y_ss, y_rs.at[v], to_y(src_y)).wait_recv()

                @pl.when(src_y == y)
                def _():
                    pltpu.make_async_copy(yb, yr.at[v], own_s.at[4]).wait()

            both = yr[0].astype(F32) + yr[1].astype(F32)
            fc[c, x, i] = (both * (1.0 / math.sqrt(tokens))).astype(BF16)
            for d in range(1, NZ):
                za_copy(i, d).start()

    for n in range(3):
        for d in range(1, NY):
            d_copy(n, d, False).wait_recv()
        d_own[n].wait()
    trow = lax.broadcasted_iota(jnp.int32, (2 * POS, POS), 0)
    tcol = lax.broadcasted_iota(jnp.int32, (2 * POS, POS), 1)
    place = [jnp.where(trow == 2 * tcol + v, 1.0, 0.0).astype(BF16) for v in range(2)]
    homes = [
        [(ra, 0), (rb, 0), (rc, 0)],
        [(ra, HD), (rb, HD), (rc, HD)],
        [(rb, 2 * HD), (rb, 3 * HD), (rc, 2 * HD)],
    ]
    for k in range(3):
        acc = None
        for v in range(2):
            view_part = jnp.concatenate(
                [
                    ref[v * GROUPS + g][:, lane : lane + HD].astype(F32)
                    for g in range(GROUPS)
                    for ref, lane in homes[k]
                ],
                axis=1,
            ).astype(BF16)
            full = jnp.concatenate([view_part, cg[k, v]], axis=1)
            t = dot(place[v], full)
            acc = t if acc is None else acc + t
        d_ref[k] = acc.astype(BF16)

    for i, (_, src_z) in enumerate(slots):

        @pl.when(src_z != z)
        def _():
            za_copy(i, 1).wait_recv()

    def xa_copy(d, mine):
        p = x_at(d)
        piece = fc.at[c, x if mine else p]
        return remote(piece, piece, xa_ss.at[d], xa_rs.at[x if mine else p], to_scene(z, p, c))

    def ka_copy(cc, xx):
        return remote(fc.at[cc, xx], fc.at[cc, xx], ka_ss.at[xx], ka_rs.at[xx], core_peer)

    for d in range(1, NX):
        xa_copy(d, True).start()
    ka_copy(c, x).start()
    for d in (1, 3, 2):
        xa_copy(d, False).wait_recv()
        ka_copy(c, x_at(d)).start()
    for xx in range(NX):
        ka_copy(1 - c, xx).wait_recv()
    for cc in range(2):
        for xx in range(NX):
            for i in range(OWNED):
                at = 32 * i + 8 * xx
                wg_ref[at : at + 8, cc * HALF : (cc + 1) * HALF] = fc[cc, xx, i].astype(F32)

    for p in range(NY):

        @pl.when(p != y)
        def _():
            for part in q_send(p):
                part.wait_send()

    for h in range(2):
        cot_end(h)
    for d in range(1, NY):
        x_copy(d, True).wait_send()
        for n in range(3):
            d_copy(n, d, True).wait_send()
    k_copy.wait_send()
    for d in range(1, NX):
        xx_copy(d, True).wait_send()
        xa_copy(d, True).wait_send()
    for d in range(1, NZ):

        @pl.when(local_block(z_at(d)) < BLOCKS)
        def _():
            z_copy(d, True).wait_send()

    @pl.when(away)
    def _():
        y_copy.wait_send()

    for i, (_, src_z) in enumerate(slots):

        @pl.when(src_z == z)
        def _():
            for d in range(1, NZ):
                za_copy(i, d).wait_send()

    for xx in range(NX):
        ka_copy(c, xx).wait_send()


def on_device(qkv, view_counts, out_weight, out_cotangent):
    vmem = pl.BlockSpec(memory_space=pltpu.VMEM)
    hbm = pl.BlockSpec(memory_space=pltpu.HBM)
    V = pltpu.VMEM
    S = pltpu.SemaphoreType.DMA
    return pl.pallas_call(
        kernel,
        out_shape=(
            jax.ShapeDtypeStruct((3, 2 * POS, WIDTH), BF16),
            jax.ShapeDtypeStruct((WIDTH // NY, WIDTH), F32),
        ),
        in_specs=[
            pl.BlockSpec(memory_space=pltpu.SMEM), hbm, hbm, hbm,
        ],
        out_specs=(vmem, vmem),
        scratch_shapes=[
            V((3, 2 * POS, WIDTH), BF16), V((2 * POS, WIDTH), BF16), V((2, POS, HALF), BF16),
            V((GW, WIDTH), BF16), V((CROSS_W, WIDTH), BF16),
            V((NY, POS, 512), BF16), V((TV, 512), BF16),
            V((NY, POS // 2, 128), BF16), V((TV // 2, 128), BF16),
            V((2, POS, WIDTH), BF16), V((TV, WIDTH), BF16),
            V((3, 2, POS, CROSS_W), F32),
            V((NY, POS, 128), BF16), V((TV, 128), BF16),
            V((3, 2, POS, CROSS_W), BF16),
            V((HEADS, TV, HD), BF16), V((HEADS, TV, HD), BF16),
            V((HEADS, TV, HD), BF16), V((HEADS, TV, HD), BF16),
            V((HEADS, TV, TV), F32), V((HEADS, TV, TV), BF16), V((TV, TV), BF16),
            V((TV, 128), BF16), V((TV, 256), BF16), V((TV, 256), BF16),
            V((NY, POS, 128), BF16), V((NY, POS, 256), BF16), V((NY, POS, 256), BF16),
            V((320, TV), BF16),
            V((320, HALF), BF16), V((320, HALF), BF16), V((BLOCKS, NX, 8, HALF), F32),
            V((NX, BLOCKS * 8, HALF), BF16), V((NX, BLOCKS * 8, HALF), BF16),
            V((NZ, 8, HALF), F32), V((NZ, 8, HALF), BF16), V((NZ, 8, HALF), BF16),
            V((8, HALF), BF16), V((2, 8, HALF), BF16), V((2, NX, OWNED, 8, HALF), BF16),
            S((6,)), S((NY,)), S((NY,)), S((NY,)), S((NY,)),
            S((2, 6)), S((2, 6)), S((2, 2)), S((2, NY)), S((2,)),
            S((NY,)), S((NY,)),
            S((NY,)), S((NY,)), S((NY,)), S((NY,)), S((NY,)), S((NY,)), S((8,)), S, S, S((NX,)), S((NX,)),
            S((NZ,)), S((NZ,)), S, S((2,)), S((NZ,)), S((OWNED,)), S((NX,)), S((NX,)), S((NX,)), S((NX,)),
        ],
        compiler_params=pltpu.CompilerParams(
            collective_id=0, has_side_effects=True, vmem_limit_bytes=30 * 1024 * 1024
        ),
        name="layer",
    )(view_counts, *(pltpu.with_memory_space_constraint(a, pltpu.HBM) for a in (qkv, out_cotangent, out_weight)))


def solution(mesh):
    in_specs = (P(None, ("scene", "seq"), None), P("scene"), P(), P(("scene", "seq"), None))
    out_specs = (P(None, ("scene", "seq"), None), P("seq", None))
    return jax.shard_map(
        on_device, mesh=mesh, in_specs=in_specs, out_specs=out_specs, check_vma=False
    )
```
